512 devices in a mesh: dp: 4 (over y), pipe: 32 (over z_lo, x), tensor: 4 (over z_hi, core).
Axes of the slice: x: 4, y: 4, z: 16 (z_hi: 2, z_lo: 8; z = z_hi * 8 + z_lo), core: 2. Of those that a mesh axis runs over, the one named last changes fastest.
Arguments:
- hidden: bfloat16 [1536, 2048], P(('dp', 'pipe'), 'tensor'), parts along dimension 0, may hold values from -20 to 20
- weight: bfloat16 [2048, 147456], P(None, ('pipe', 'tensor')), may hold values from -16 to 16
- targets: int32 [1536], P('dp'), parts along dimension 0, may hold values from 0 to 147455
- row_weight: float32 [1536], P('dp'), parts along dimension 0, may hold values from 2 to 20
Outputs:
- grad_hidden: bfloat16 [1536, 2048], P(('dp', 'pipe'), 'tensor'), parts along dimension 0
- row_loss: float32 [1536], P('dp'), parts along dimension 0
The draws below stay inside these ranges and needn't reach their ends.
There are 4 independent parts, one for each index of `dp`. The reference program is written for one: setup_inputs(seed, part) draws one part's arguments, and reference() takes and returns one part's arrays. A program takes and returns all parts, laid end to end along the dimension named above; an argument that names none is the same for every part. Nothing has to cross between parts.
All inputs are finite; a program needn't handle non-finite values.
Results may differ from the reference program's by a relative error of at most 0.0051.
Values may be sent and summed in bfloat16 or wider, within the bound.
A program may use at most 64 MiB of HBM per device.

```python
import math
import jax
import jax.numpy as jnp
from jax import lax

D = 2048
ROWS = 384
VOCAB = 147456


def draw_hidden(key, part):
    first_key = jax.random.fold_in(key, 0)
    values = jnp.clip(jax.random.normal(first_key, (ROWS, D), jnp.float32), -6.0, 6.0)
    return values.astype(jnp.bfloat16)


def draw_weight(key, part):
    spread = 3.0 / math.sqrt(D)
    values = jnp.clip(jax.random.normal(key, (D, VOCAB), jnp.float32), -6.0, 6.0) * spread
    return values.astype(jnp.bfloat16)


def set_ends(result, rng, smallest, largest):
    longest = result.shape.index(max(result.shape))
    spots = []
    for shift in (0, 1):
        where = [jax.random.randint(jax.random.fold_in(rng, axis), (), 0, length) for axis, length in enumerate(result.shape)]
        where[longest] = (where[longest] + shift) % result.shape[longest]
        spots.append(tuple(where))
    return result.at[spots[0]].set(smallest).at[spots[1]].set(largest)


def setup_inputs(seed: int = 0, part: int = 0) -> dict:
    seeds = jax.random.split(jax.random.key(seed), 5)
    part_keys = jax.random.split(jax.random.fold_in(seeds[4], part), 5)
    hidden = draw_hidden(jax.random.fold_in(jax.random.fold_in(seeds[4], part), 71), part)
    weight = draw_weight(jax.random.fold_in(seeds[4], 71), part)
    targets = set_ends(jax.random.randint(part_keys[2], (ROWS,), 0, VOCAB), jax.random.fold_in(part_keys[2], 1), 0, VOCAB - 1).astype(jnp.int32)
    row_weight = jnp.clip(jnp.exp(jax.random.uniform(part_keys[3], (ROWS,), jnp.float32, math.log(2.0), math.log(20.0))), 2.0, 20.0)
    return dict(hidden=hidden, weight=weight, targets=targets, row_weight=row_weight)


def reference(hidden, weight, targets, row_weight):
    logits = jnp.dot(hidden, weight, preferred_element_type=jnp.float32)
    row_max = jnp.max(logits, axis=1)
    shifted = jnp.exp(logits - row_max[:, None])
    sum_exp = jnp.sum(shifted, axis=1)
    is_target = lax.broadcasted_iota(jnp.int32, logits.shape, 1) == targets[:, None].astype(jnp.int32)
    label_logit = jnp.sum(jnp.where(is_target, logits, jnp.zeros_like(logits)), axis=1)
    row_loss = jnp.log(sum_exp) + row_max - label_logit
    dlogits = (row_weight[:, None] * (shifted / sum_exp[:, None] - is_target.astype(logits.dtype))).astype(jnp.bfloat16)
    grad_hidden = lax.dot_general(dlogits, weight, (((1,), (1,)), ((), ())), preferred_element_type=jnp.float32)
    return grad_hidden.astype(jnp.bfloat16), row_loss
```

```python
import functools

import jax
import jax.numpy as jnp
from jax import lax
from jax.experimental import pallas as pl
from jax.experimental.pallas import tpu as pltpu
from jax.sharding import Mesh
from jax.sharding import PartitionSpec as P

AXES = ("dp", "zlo", "x", "zhi", "core")
MESH = pl.DeviceIdType.MESH
F32 = jnp.float32
BF16 = jnp.bfloat16
LANES = 128
TILE = 256


def kernel(
    dims, h_ref, w_hbm, t_ref, rw_ref, out_ref, loss_ref,
    w_ref, w_sem, hid, xin, asm, x1_s, x1_r, zr_s, zr_r, zl_s, zl_r, x2_s, x2_r, cg_s, cg_r,
    logits, dlog, tcol, stat, srow, s_core, s_x, s_z, sc_s, sc_r, sx_s, sx_r, sz_s, sz_r,
    c_out, c_in, rc_s, rc_r, x_out, x_in, x_own, rx_s, rx_r, z_out, z_in, z_own, rz_s, rz_r,
    f_out, f_in, rf_s, rf_r,
):
    nzlo, nx = dims
    nz = 2 * nzlo
    rb = h_ref.shape[0]
    rows = nzlo * nx * rb
    zrows = nx * rb
    vocab = w_ref.shape[1]
    zlo, x = lax.axis_index("zlo"), lax.axis_index("x")
    zhi, core = lax.axis_index("zhi"), lax.axis_index("core")
    z = zhi * nzlo + zlo
    other = 1 - core

    def at_z(k):
        k = lax.rem(k + nz, nz)
        return {"zhi": k // nzlo, "zlo": lax.rem(k, nzlo)}

    def at_x(k):
        return {"x": lax.rem(k, nx)}

    at_core = {"core": other}

    def remote(src, dst, send, recv, where):
        return pltpu.make_async_remote_copy(
            src_ref=src, dst_ref=dst, send_sem=send, recv_sem=recv, device_id=where, device_id_type=MESH
        )

    barrier = pltpu.get_barrier_semaphore()
    near = [at_core, at_z(z + 1), at_z(z - 1)] + [at_x(x + d) for d in range(1, nx)]
    for where in near:
        pl.semaphore_signal(barrier, inc=1, device_id=where, device_id_type=MESH)
    w_copy = pltpu.make_async_copy(w_hbm, w_ref, w_sem)
    w_copy.start()

    srow[...] = jnp.zeros_like(srow)
    srow[0:1, :] = t_ref[...].astype(F32)
    srow[1:2, :] = rw_ref[...]
    tcol[...] = jnp.transpose(srow[...], (1, 0))
    pl.semaphore_wait(barrier, len(near))

    x1 = []
    for d in range(1, nx):
        q = lax.rem(x + d, nx)
        lanes = pl.ds(pl.multiple_of(q * LANES, LANES), LANES)
        x1.append(remote(h_ref.at[:, lanes], xin.at[x], x1_s.at[d - 1], x1_r.at[d - 1], at_x(q)))
        x1[-1].start()
    xin[x] = h_ref[:, pl.ds(pl.multiple_of(x * LANES, LANES), LANES)]
    for copy in x1:
        copy.wait()
    for j in range(nx):
        asm[j * rb : (j + 1) * rb, :] = xin[j].astype(F32)

    def block(k):
        k = lax.rem(k + nz, nz)
        return k // nzlo, pl.ds(pl.multiple_of(lax.rem(k, nzlo) * zrows, zrows), zrows)

    def piece(k, chunk):
        half, span = block(k)
        return hid.at[half * 2 * nx + chunk, span, :]

    mine = core * nx + x
    half_z, span_z = block(z)
    hid[half_z * 2 * nx + mine, span_z, :] = asm[...].astype(BF16)

    def right(s):
        return remote(piece(z - s, mine), piece(z - s, mine), zr_s.at[s], zr_r.at[s], at_z(z + 1))

    def left(s):
        return remote(piece(z + s, mine), piece(z + s, mine), zl_s.at[s], zl_r.at[s], at_z(z - 1))

    def over_x(k, d):
        n = lax.rem(k + nz, nz)
        return remote(piece(k, mine), piece(k, mine), x2_s.at[n, d - 1], x2_r.at[n, d - 1], at_x(x + d))

    def over_core(k):
        n = lax.rem(k + nz, nz)
        half, span = block(k)
        both = hid.at[pl.ds(half * 2 * nx + core * nx, nx), span, :]
        return remote(both, both, cg_s.at[n], cg_r.at[n], at_core)

    def start_x(k):
        for d in range(1, nx):
            over_x(k, d).start()

    def pass_to_core(k):
        for d in range(1, nx):
            over_x(k, d).wait_recv()
        over_core(k).start()

    right(0).start()
    left(0).start()
    start_x(z)
    right(0).wait_recv()

    @pl.loop(1, nz // 2)
    def _(s):
        right(s).start()
        left(s - 1).wait_recv()

        @pl.when(s < nz // 2 - 1)
        def _():
            left(s).start()

        start_x(z - s)
        start_x(z + s)
        pass_to_core(z - s + 1)

        @pl.when(s > 1)
        def _():
            pass_to_core(z + s - 1)

        right(s).wait_recv()

    start_x(z + nz // 2)
    pass_to_core(z - nz // 2 + 1)
    if nz > 2:
        pass_to_core(z + nz // 2 - 1)
    pass_to_core(z + nz // 2)
    w_copy.wait()

    @pl.loop(0, nz)
    def _(k):
        over_core(k).wait()
        for d in range(1, nx):
            over_x(k, d).wait_send()

    @pl.loop(0, nz // 2)
    def _(s):
        right(s).wait_send()

    @pl.loop(0, nz // 2 - 1)
    def _(s):
        left(s).wait_send()

    chunks = 4 * nx

    def all_rows():
        return jnp.concatenate([hid[k] for k in range(chunks)], axis=1)

    @pl.loop(0, vocab // TILE)
    def _(n):
        cols = pl.ds(pl.multiple_of(n * TILE, TILE), TILE)
        logits[:, cols] = jnp.dot(all_rows(), w_ref[:, cols], preferred_element_type=F32)

    if vocab % TILE:
        logits[:, vocab // TILE * TILE :] = jnp.dot(
            all_rows(), w_ref[:, vocab // TILE * TILE :], preferred_element_type=F32
        )

    offset = ((zlo * nx + x) * 4 + zhi * 2 + core) * vocab
    lane = lax.broadcasted_iota(jnp.int32, (zrows, LANES), 1)
    column = lax.broadcasted_iota(jnp.int32, (zrows, vocab), 1)

    def is_target(span):
        wanted = tcol[span, 0:1].astype(jnp.int32) - offset
        return column == wanted

    @pl.loop(0, nzlo)
    def _(r):
        span = pl.ds(pl.multiple_of(r * zrows, zrows), zrows)
        part = logits[span, :]
        top = jnp.max(part, axis=1, keepdims=True)
        summed = jnp.sum(jnp.exp(part - top), axis=1, keepdims=True)
        label = jnp.sum(jnp.where(is_target(span), part, 0.0), axis=1, keepdims=True)
        stat[span, :] = jnp.where(lane == 0, top, jnp.where(lane == 1, summed, jnp.where(lane == 2, label, 0.0)))

    def joined(slots):
        tops = slots[:, 0:1, :]
        top = jnp.max(tops, axis=0)
        summed = jnp.sum(slots[:, 1:2, :] * jnp.exp(tops - top[None]), axis=0)
        return top, summed, jnp.sum(slots[:, 2:3, :], axis=0)

    def put(slot, values):
        for k, value in enumerate(values):
            slot[k : k + 1, :] = value
        slot[3:4, :] = jnp.zeros_like(values[0])

    flipped = jnp.transpose(stat[...], (1, 0))
    s_core[core] = flipped[0:4, :]
    copy = remote(s_core.at[core], s_core.at[core], sc_s, sc_r, at_core)
    copy.start()
    copy.wait()
    put(s_x.at[x], joined(s_core[...]))
    copies = [
        remote(s_x.at[x], s_x.at[x], sx_s.at[d - 1], sx_r.at[d - 1], at_x(x + d)) for d in range(1, nx)
    ]
    for copy in copies:
        copy.start()
    for copy in copies:
        copy.wait()
    put(s_z.at[z], joined(s_x[...]))

    def stats_z(d):
        return remote(s_z.at[z], s_z.at[z], sz_s.at[d], sz_r.at[d], at_z(z + d))

    @pl.loop(1, nz)
    def _(d):
        stats_z(d).start()

    @pl.loop(1, nz)
    def _(d):
        stats_z(d).wait()

    top, summed, label = joined(s_z[...])
    loss_ref[...] = jnp.log(summed) + top - label
    srow[0:1, :] = top
    srow[1:2, :] = 1.0 / summed
    stat[...] = jnp.transpose(srow[...], (1, 0))

    @pl.loop(0, nzlo)
    def _(r):
        span = pl.ds(pl.multiple_of(r * zrows, zrows), zrows)
        shifted = jnp.exp(logits[span, :] - stat[span, 0:1])
        soft = shifted * stat[span, 1:2] - is_target(span).astype(F32)
        dlog[span, :] = (tcol[span, 1:2] * soft).astype(BF16)

    def product(half, who, pair):
        first = (half * 2 + who) * nx * LANES + pair * TILE
        part = w_ref[pl.ds(pl.multiple_of(first, TILE), TILE), :]
        return lax.dot_general(dlog[...], part, (((1,), (1,)), ((), ())), preferred_element_type=F32)

    pairs = nx // 2

    def to_core(n):
        two = pl.ds(2 * n, 2)
        return remote(c_out.at[two], c_in.at[two], rc_s.at[n], rc_r.at[n], at_core)

    @pl.loop(0, 2 * pairs)
    def _(n):
        part = product(n // pairs, other, lax.rem(n, pairs))
        c_out[2 * n] = part[:, :LANES].astype(BF16)
        c_out[2 * n + 1] = part[:, LANES:].astype(BF16)
        to_core(n).start()

    def to_x(half, d):
        q = lax.rem(x + d, nx)
        return remote(
            x_out.at[half * nx + q], x_in.at[half * (nx - 1) + d - 1],
            rx_s.at[half, d - 1], rx_r.at[half, d - 1], at_x(q),
        )

    @pl.loop(0, 2)
    def _(half):
        @pl.loop(0, pairs)
        def _(pair):
            n = half * pairs + pair
            part = product(half, core, pair)
            to_core(n).wait_recv()
            for k in range(2):
                whole = part[:, k * LANES : (k + 1) * LANES] + c_in[2 * n + k].astype(F32)
                x_out[2 * n + k] = whole.astype(BF16)

                @pl.when(2 * pair + k == x)
                def _():
                    x_own[half] = whole

        for d in range(1, nx):
            to_x(half, d).start()

    def to_z(half, low):
        span = pl.ds(pl.multiple_of(low * zrows, zrows), zrows)
        return remote(
            z_out.at[half, span, :], z_in.at[z], rz_s.at[half * nzlo + low], rz_r.at[z],
            {"zhi": half, "zlo": low},
        )

    @pl.loop(0, 2)
    def _(half):
        for d in range(1, nx):
            to_x(half, d).wait_recv()
        whole = x_own[half]
        for d in range(1, nx):
            whole += x_in[half * (nx - 1) + d - 1].astype(F32)
        z_out[half] = whole.astype(BF16)

        @pl.when(half == zhi)
        def _():
            z_own[...] = whole

        @pl.loop(0, nzlo)
        def _(low):
            @pl.when(half * nzlo + low != z)
            def _():
                to_z(half, low).start()

    total = z_own[span_z, :]
    asm[...] = total

    @pl.loop(0, nz)
    def _(k):
        @pl.when(k != z)
        def _():
            remote(z_in.at[k], z_in.at[k], rz_s.at[k], rz_r.at[k], at_core).wait_recv()
            asm[...] += z_in[k].astype(F32)

    for j in range(nx):
        f_out[j] = asm[j * rb : (j + 1) * rb, :].astype(BF16)
    f_in[x] = f_out[x]
    copies = [
        remote(f_out.at[lax.rem(x + d, nx)], f_in.at[x], rf_s.at[d - 1], rf_r.at[d - 1], at_x(x + d))
        for d in range(1, nx)
    ]
    for copy in copies:
        copy.start()
    for copy in copies:
        copy.wait()
    for q in range(nx):
        out_ref[:, q * LANES : (q + 1) * LANES] = f_in[q]

    @pl.loop(0, 2 * pairs)
    def _(n):
        to_core(n).wait_send()

    @pl.loop(0, 2)
    def _(half):
        for d in range(1, nx):
            to_x(half, d).wait_send()

        @pl.loop(0, nzlo)
        def _(low):
            @pl.when(half * nzlo + low != z)
            def _():
                to_z(half, low).wait_send()


def per_device(dims, hidden, weight, targets, row_weight):
    nzlo, nx = dims
    nz = 2 * nzlo
    rb, wide = hidden.shape
    depth, vocab = weight.shape
    rows = targets.shape[0]
    zrows = nx * rb
    vmem, dma = pltpu.VMEM, pltpu.SemaphoreType.DMA
    spec = pl.BlockSpec(memory_space=pltpu.VMEM)
    scratch = [
        vmem((depth, vocab), BF16), dma(()),
        vmem((4 * nx, rows, LANES), BF16), vmem((nx, rb, LANES), BF16), vmem((zrows, LANES), F32),
        dma((nx - 1,)), dma((nx - 1,)),
        dma((nz,)), dma((nz,)), dma((nz,)), dma((nz,)),
        dma((nz, nx - 1)), dma((nz, nx - 1)), dma((nz,)), dma((nz,)),
        vmem((rows, vocab), F32), vmem((rows, vocab), BF16), vmem((rows, LANES), F32),
        vmem((rows, LANES), F32), vmem((LANES, rows), F32),
        vmem((2, 4, rows), F32), vmem((nx, 4, rows), F32), vmem((nz, 4, rows), F32),
        dma(()), dma(()), dma((nx - 1,)), dma((nx - 1,)), dma((nz,)), dma((nz,)),
        vmem((2 * nx, rows, LANES), BF16), vmem((2 * nx, rows, LANES), BF16), dma((nx,)), dma((nx,)),
        vmem((2 * nx, rows, LANES), BF16), vmem((2 * (nx - 1), rows, LANES), BF16), vmem((2, rows, LANES), F32),
        dma((2, nx - 1)), dma((2, nx - 1)),
        vmem((2, rows, LANES), BF16), vmem((nz, zrows, LANES), BF16), vmem((rows, LANES), F32),
        dma((nz,)), dma((nz,)),
        vmem((nx, rb, LANES), BF16), vmem((nx, rb, LANES), BF16), dma((nx - 1,)), dma((nx - 1,)),
    ]
    grad, loss = pl.pallas_call(
        functools.partial(kernel, dims),
        out_shape=(
            jax.ShapeDtypeStruct((rb, wide), BF16),
            jax.ShapeDtypeStruct((1, rows), F32),
        ),
        in_specs=[spec, pl.BlockSpec(memory_space=pl.ANY), spec, spec],
        out_specs=(spec, spec),
        scratch_shapes=scratch,
        compiler_params=pltpu.CompilerParams(collective_id=0, has_side_effects=True),
    )(hidden, weight, targets.reshape(1, rows), row_weight.reshape(1, rows))
    return grad, loss.reshape(rows)


def on_mesh(split):
    dims = (split.shape["zlo"], split.shape["x"])
    tensor, pipe = ("zhi", "core"), ("zlo", "x")
    in_specs = (P(("dp", *pipe), tensor), P(None, (*pipe, *tensor)), P("dp"), P("dp"))
    out_specs = (P(("dp", *pipe), tensor), P("dp"))
    return jax.shard_map(
        functools.partial(per_device, dims), mesh=split, in_specs=in_specs, out_specs=out_specs, check_vma=False
    )


def solution(mesh):
    return on_mesh(Mesh(mesh.devices.reshape(mesh.shape["dp"], 8, 4, 2, 2), AXES))
```

```python
import functools

import jax
import jax.numpy as jnp
from jax import lax
from jax.experimental import pallas as pl
from jax.experimental.pallas import tpu as pltpu
from jax.sharding import Mesh
from jax.sharding import PartitionSpec as P

AXES = ("dp", "zlo", "x", "zhi", "core")
MESH = pl.DeviceIdType.MESH
F32 = jnp.float32
BF16 = jnp.bfloat16
LANES = 128
TILE = 256


def kernel(
    dims, h_ref, w_hbm, t_ref, rw_ref, out_ref, loss_ref,
    w_ref, w_sem, hid, pieces, tall, wide_rows, zg_s, zg_r, xg_s, xg_r, cg_s, cg_r,
    logits, soft, tcol, stat, srow, s_core, s_x, s_z, sc_s, sc_r, sx_s, sx_r, sz_s, sz_r,
    t_out, t_in, t_own, tx_in, tc_s, tc_r, tx_s, tx_r,
    c_out, c_in, rc_s, rc_r, whole_ref, x_out, x_in, x_own, rx_s, rx_r,
    acc, z_out, z_in, rz_s, rz_r,
):
    nzlo, nx = dims
    nz = 2 * nzlo
    rb, wide = h_ref.shape
    quarters = wide // LANES
    rows = nzlo * nx * rb
    xrows = nzlo * rb
    step = 48
    vocab = w_ref.shape[1]
    zlo, x = lax.axis_index("zlo"), lax.axis_index("x")
    zhi, core = lax.axis_index("zhi"), lax.axis_index("core")
    z = zhi * nzlo + zlo
    other = 1 - core
    pairs = wide // TILE

    def at_z(k):
        k = lax.rem(k + nz, nz)
        return {"zhi": k // nzlo, "zlo": lax.rem(k, nzlo)}

    def at_x(k):
        return {"x": lax.rem(k, nx)}

    at_core = {"core": other}

    def remote(src, dst, send, recv, where):
        return pltpu.make_async_remote_copy(
            src_ref=src, dst_ref=dst, send_sem=send, recv_sem=recv, device_id=where, device_id_type=MESH
        )

    def rows_of(k, size):
        return pl.ds(pl.multiple_of(k * size, size), size)

    barrier = pltpu.get_barrier_semaphore()
    partners = [at_z(z + d) for d in range(1, nz)] + [at_x(x + d) for d in range(1, nx)] + [at_core]
    for where in partners:
        pl.semaphore_signal(barrier, inc=1, device_id=where, device_id_type=MESH)
    w_copy = pltpu.make_async_copy(w_hbm, w_ref, w_sem)
    w_copy.start()

    srow[...] = jnp.zeros_like(srow)
    srow[0:1, :] = t_ref[...].astype(F32).reshape(1, rows)
    srow[1:2, :] = rw_ref[...].reshape(1, rows)
    stat[...] = jnp.transpose(srow[...], (1, 0))
    for i in range(nx):
        for j in range(nzlo):
            to, of = (i * nzlo + j) * rb, (j * nx + i) * rb
            tcol[to : to + rb, :] = stat[of : of + rb, :]

    for j in range(quarters):
        tall[0, j * rb : (j + 1) * rb, :] = h_ref[:, j * LANES : (j + 1) * LANES].astype(F32)
    pieces[z] = tall[0].astype(BF16)

    offset = ((zlo * nx + x) * 4 + zhi * 2 + core) * vocab
    lane = lax.broadcasted_iota(jnp.int32, (step, LANES), 1)
    column = lax.broadcasted_iota(jnp.int32, (step, vocab), 1)

    def is_target(span):
        wanted = tcol[span, 0:1].astype(jnp.int32) - offset
        return column == wanted

    @pl.loop(0, rows // step)
    def _(r):
        span = rows_of(r, step)
        soft[span, :] = jnp.where(is_target(span), 1.0, 0.0).astype(BF16)

    def product(half, who, pair):
        first = (half * 2 + who) * wide + pair * TILE
        part = w_ref[pl.ds(pl.multiple_of(first, TILE), TILE), :]
        return lax.dot_general(soft[...], part, (((1,), (1,)), ((), ())), preferred_element_type=F32)

    def tile(pair):
        return rows_of(pair, TILE)

    w_copy.wait()

    @pl.loop(0, 2 * pairs)
    def _(n):
        half, pair = n // pairs, lax.rem(n, pairs)
        t_out[half, :, tile(pair)] = product(half, other, pair).astype(BF16)
        t_own[half, :, tile(pair)] = product(half, core, pair).astype(BF16)

    pl.semaphore_wait(barrier, len(partners))

    def gather_z(d):
        k = lax.rem(z + d + nz, nz)
        return remote(pieces.at[z], pieces.at[z], zg_s.at[k], zg_r.at[z], at_z(z + d))

    for d in range(1, nz // 2):
        gather_z(d).start()
        gather_z(-d).start()
    gather_z(nz // 2).start()

    def t_core(half):
        return remote(t_out.at[half], t_in.at[half], tc_s.at[half], tc_r.at[half], at_core)

    t_core(0).start()
    t_core(1).start()

    size = min(4, nzlo)
    groups = nz // size
    grows = size * rb
    per_half = groups // 2

    def place(g, chunk_x):
        first = chunk_x * xrows + lax.rem(g, per_half) * grows
        return hid.at[(g // per_half) * 2 + core, pl.ds(pl.multiple_of(first, grows), grows), :]

    def over_x(g, d):
        return remote(place(g, x), place(g, x), xg_s.at[g, d - 1], xg_r.at[g, d - 1], at_x(x + d))

    def over_core(g, d):
        whose = lax.rem(x + d, nx)
        return remote(place(g, whose), place(g, whose), cg_s.at[g, d], cg_r.at[g, d], at_core)

    def pass_to_core(g):
        for d in range(1, nx):
            over_x(g, nx - d).wait_recv()
            over_core(g, d).start()

    def take_group(g):
        for i in range(size):
            k = g * size + i

            @pl.when(k != z)
            def _():
                remote(pieces.at[k], pieces.at[k], zg_s.at[k], zg_r.at[k], at_core).wait_recv()

            tall[i] = pieces[k].astype(F32)
            for j in range(quarters):
                wide_rows[i * rb : (i + 1) * rb, j * LANES : (j + 1) * LANES] = tall[i, j * rb : (j + 1) * rb, :]
        first = x * xrows + lax.rem(g, per_half) * grows
        hid[(g // per_half) * 2 + core, pl.ds(pl.multiple_of(first, grows), grows), :] = wide_rows[...].astype(BF16)
        for d in range(1, nx):
            over_x(g, d).start()
        over_core(g, 0).start()

    def in_turn(i):
        if groups == 2:
            return lax.rem(z // size + i, groups)
        shift = jnp.where(i == 2, 3, jnp.where(i == 3, 2, i))
        return lax.rem(z // size + shift, groups)

    @pl.loop(0, groups)
    def _(i):
        take_group(in_turn(i))

        @pl.when(i > 0)
        def _():
            pass_to_core(in_turn(i - 1))

    def t_over_x(half, d):
        q = lax.rem(x + d, nx)
        return remote(
            t_own.at[half, rows_of(q, xrows), :], tx_in.at[d - 1, half], tx_s.at[half, d - 1], tx_r.at[half, d - 1], at_x(q)
        )

    for half in range(2):
        t_core(half).wait_recv()

        @pl.loop(0, rows // step)
        def _(r):
            span = rows_of(r, step)
            t_own[half, span, :] = (t_own[half, span, :].astype(F32) + t_in[half, span, :].astype(F32)).astype(BF16)

    pass_to_core(in_turn(groups - 1))

    for half in range(2):
        for d in range(1, nx):
            t_over_x(half, d).start()

    @pl.loop(0, groups)
    def _(g):
        for d in range(nx):
            over_core(g, d).wait_recv()

    def all_rows():
        return jnp.concatenate([hid[k] for k in range(4)], axis=1)

    @pl.loop(0, vocab // TILE)
    def _(n):
        cols = tile(n)
        logits[:, cols] = jnp.dot(all_rows(), w_ref[:, cols], preferred_element_type=F32)

    if vocab % TILE:
        logits[:, vocab // TILE * TILE :] = jnp.dot(
            all_rows(), w_ref[:, vocab // TILE * TILE :], preferred_element_type=F32
        )

    @pl.loop(0, rows // step)
    def _(r):
        span = rows_of(r, step)
        part = logits[span, :]
        top = jnp.max(part, axis=1, keepdims=True)
        shifted = jnp.exp(part - top)
        soft[span, :] = shifted.astype(BF16)
        summed = jnp.sum(shifted, axis=1, keepdims=True)
        label = jnp.sum(jnp.where(is_target(span), part, 0.0), axis=1, keepdims=True)
        stat[span, :] = jnp.where(lane == 0, top, jnp.where(lane == 1, summed, jnp.where(lane == 2, label, 0.0)))

    def joined(slots):
        tops = slots[:, 0:1, :]
        top = jnp.max(tops, axis=0)
        summed = jnp.sum(slots[:, 1:2, :] * jnp.exp(tops - top[None]), axis=0)
        return top, summed, jnp.sum(slots[:, 2:3, :], axis=0)

    def put(slot, values):
        for k, value in enumerate(values):
            slot[k : k + 1, :] = value
        slot[3:4, :] = jnp.zeros_like(values[0])

    flipped = jnp.transpose(stat[...], (1, 0))
    s_core[core] = flipped[0:4, :]
    stats_core = remote(s_core.at[core], s_core.at[core], sc_s, sc_r, at_core)
    stats_core.start()

    def to_core(half, pair):
        n = half * pairs + pair
        part = c_out.at[half, :, tile(pair)]
        return remote(part, c_in.at[half, :, tile(pair)], rc_s.at[n], rc_r.at[n], at_core)

    def for_partner(half):
        @pl.loop(0, pairs)
        def _(pair):
            c_out[half, :, tile(pair)] = product(half, other, pair).astype(BF16)
            to_core(half, pair).start()

    for_partner(0)
    stats_core.wait()
    put(s_x.at[x], joined(s_core[...]))
    stats_x = [
        remote(s_x.at[x], s_x.at[x], sx_s.at[d - 1], sx_r.at[d - 1], at_x(x + d)) for d in range(1, nx)
    ]
    for copy in stats_x:
        copy.start()
    core_top = s_x[x, 0:1, :]
    srow[0:1, :] = jnp.exp(s_core[core, 0:1, :] - core_top)
    srow[1:2, :] = jnp.exp(s_core[other, 0:1, :] - core_top)
    stat[...] = jnp.transpose(srow[...], (1, 0))
    for_partner(1)

    def to_x(half, pair, d):
        q = lax.rem(x + d, nx)
        n = half * pairs + pair
        return remote(
            x_out.at[half, rows_of(q, xrows), tile(pair)], x_in.at[d - 1, half, :, tile(pair)],
            rx_s.at[n, d - 1], rx_r.at[n, d - 1], at_x(q),
        )

    @pl.loop(0, 2 * pairs)
    def _(n):
        half, pair = n // pairs, lax.rem(n, pairs)
        whole_ref[...] = product(half, core, pair)
        to_core(half, pair).wait_recv()

        @pl.loop(0, rows // step)
        def _(r):
            span = rows_of(r, step)
            got = c_in[half, span, tile(pair)].astype(F32)
            whole = whole_ref[span, :] * stat[span, 0:1] + got * stat[span, 1:2]
            whole_ref[span, :] = whole
            x_out[half, span, tile(pair)] = whole.astype(BF16)

        x_own[half, :, tile(pair)] = whole_ref[rows_of(x, xrows), :]
        for d in range(1, nx):
            to_x(half, pair, d).start()

    for copy in stats_x:
        copy.wait()
    put(s_z.at[z], joined(s_x[...]))

    def stats_z(d):
        return remote(s_z.at[z], s_z.at[z], sz_s.at[d], sz_r.at[d], at_z(z + d))

    @pl.loop(1, nz)
    def _(d):
        stats_z(d).start()

    x_top = s_z[z, 0:1, :]
    srow[0:1, :] = jnp.exp(s_x[x, 0:1, :] - x_top)
    for d in range(1, nx):
        srow[d : d + 1, :] = jnp.exp(s_x[lax.rem(x + nx - d, nx), 0:1, :] - x_top)
    stat[...] = jnp.transpose(srow[...], (1, 0))
    own_rows = rows_of(x, xrows)

    @pl.loop(0, 2)
    def _(half):
        for d in range(1, nx):
            for pair in range(pairs):
                to_x(half, pair, d).wait_recv()
        whole = x_own[half] * stat[own_rows, 0:1]
        for d in range(1, nx):
            whole += x_in[d - 1, half].astype(F32) * stat[own_rows, d : d + 1]
        acc[half] = whole

    @pl.loop(1, nz)
    def _(d):
        stats_z(d).wait()

    top, summed, label = joined(s_z[...])
    srow[0:1, :] = jnp.exp(x_top - top) / summed
    srow[1:2, :] = jnp.log(summed) + top - label
    stat[...] = jnp.transpose(srow[...], (1, 0))

    def to_z(k):
        return remote(z_out.at[k], z_in.at[z], rz_s.at[k], rz_r.at[z], at_z(k))

    @pl.loop(0, 2)
    def _(half):
        weight = tcol[own_rows, 1:2]
        hit = t_own[half, own_rows, :].astype(F32)
        for d in range(1, nx):
            t_over_x(half, d).wait_recv()
            hit += tx_in[d - 1, half].astype(F32)
        acc[half] = acc[half] * (weight * stat[own_rows, 0:1]) - weight * hit
        for low in range(nzlo):
            slot = low % 4
            for j in range(quarters):
                tall[slot, j * rb : (j + 1) * rb, :] = acc[half, low * rb : (low + 1) * rb, j * LANES : (j + 1) * LANES]
            k = half * nzlo + low

            @pl.when(k == z)
            def _():
                tall[4] = tall[slot]

            @pl.when(k != z)
            def _():
                z_out[k] = tall[slot].astype(BF16)
                to_z(k).start()

    for i in range(nx):
        for j in range(nzlo):
            of, to = (i * nzlo + j) * rb, (j * nx + i) * rb
            logits[to : to + rb, 0:LANES] = stat[of : of + rb, :]
    loss_ref[...] = jnp.transpose(logits[:, 0:LANES], (1, 0))[1:2, :].reshape(rows)

    @pl.loop(0, nz)
    def _(k):
        @pl.when(k != z)
        def _():
            remote(z_in.at[k], z_in.at[k], rz_s.at[k], rz_r.at[k], at_core).wait_recv()
            tall[4] += z_in[k].astype(F32)

    for j in range(quarters):
        out_ref[:, j * LANES : (j + 1) * LANES] = tall[4, j * rb : (j + 1) * rb, :].astype(BF16)

    @pl.loop(1, nz)
    def _(d):
        gather_z(d).wait_send()
        to_z(lax.rem(z + d, nz)).wait_send()

    @pl.loop(0, groups)
    def _(g):
        over_core(g, 0).wait_send()
        for d in range(1, nx):
            over_core(g, d).wait_send()
            over_x(g, d).wait_send()

    @pl.loop(0, 2)
    def _(half):
        t_core(half).wait_send()
        for d in range(1, nx):
            t_over_x(half, d).wait_send()
        for pair in range(pairs):
            to_core(half, pair).wait_send()
            for d in range(1, nx):
                to_x(half, pair, d).wait_send()


def per_device(dims, hidden, weight, targets, row_weight):
    nzlo, nx = dims
    nz = 2 * nzlo
    rb, wide = hidden.shape
    depth, vocab = weight.shape
    rows = targets.shape[0]
    xrows = nzlo * rb
    size = min(4, nzlo)
    groups = nz // size
    tallness = rb * wide // LANES
    pairs = wide // TILE
    vmem, dma = pltpu.VMEM, pltpu.SemaphoreType.DMA
    spec = pl.BlockSpec(memory_space=pltpu.VMEM)
    halves = vmem((2, rows, wide), BF16)
    scratch = [
        vmem((depth, vocab), BF16), dma(()),
        vmem((4, rows, wide), BF16), vmem((nz, tallness, LANES), BF16), vmem((5, tallness, LANES), F32),
        vmem((size * rb, wide), F32),
        dma((nz,)), dma((nz,)), dma((groups, nx - 1)), dma((groups, nx - 1)), dma((groups, nx)), dma((groups, nx)),
        vmem((rows, vocab), F32), vmem((rows, vocab), BF16), vmem((rows, LANES), F32),
        vmem((rows, LANES), F32), vmem((LANES, rows), F32),
        vmem((2, 4, rows), F32), vmem((nx, 4, rows), F32), vmem((nz, 4, rows), F32),
        dma(()), dma(()), dma((nx - 1,)), dma((nx - 1,)), dma((nz,)), dma((nz,)),
        halves, halves, halves, vmem((nx - 1, 2, xrows, wide), BF16),
        dma((2,)), dma((2,)), dma((2, nx - 1)), dma((2, nx - 1)),
        halves, halves, dma((2 * pairs,)), dma((2 * pairs,)), vmem((rows, TILE), F32),
        halves, vmem((nx - 1, 2, xrows, wide), BF16), vmem((2, xrows, wide), F32),
        dma((2 * pairs, nx - 1)), dma((2 * pairs, nx - 1)),
        vmem((2, xrows, wide), F32), vmem((nz, tallness, LANES), BF16), vmem((nz, tallness, LANES), BF16),
        dma((nz,)), dma((nz,)),
    ]
    return pl.pallas_call(
        functools.partial(kernel, dims),
        out_shape=(
            jax.ShapeDtypeStruct((rb, wide), BF16),
            jax.ShapeDtypeStruct((rows,), F32),
        ),
        in_specs=[spec, pl.BlockSpec(memory_space=pl.ANY), spec, spec],
        out_specs=(spec, spec),
        scratch_shapes=scratch,
        compiler_params=pltpu.CompilerParams(collective_id=0, has_side_effects=True),
    )(hidden, weight, targets, row_weight)


def on_mesh(split):
    dims = (split.shape["zlo"], split.shape["x"])
    tensor, pipe = ("zhi", "core"), ("zlo", "x")
    in_specs = (P(("dp", *pipe), tensor), P(None, (*pipe, *tensor)), P("dp"), P("dp"))
    out_specs = (P(("dp", *pipe), tensor), P("dp"))
    return jax.shard_map(
        functools.partial(per_device, dims), mesh=split, in_specs=in_specs, out_specs=out_specs, check_vma=False
    )


def solution(mesh):
    return on_mesh(Mesh(mesh.devices.reshape(mesh.shape["dp"], 8, 4, 2, 2), AXES))
```

```python
import functools

import jax
import jax.numpy as jnp
from jax import lax
from jax.experimental import pallas as pl
from jax.experimental.pallas import tpu as pltpu
from jax.sharding import Mesh
from jax.sharding import PartitionSpec as P

AXES = ("dp", "zlo", "x", "zhi", "core")
MESH = pl.DeviceIdType.MESH
F32 = jnp.float32
BF16 = jnp.bfloat16
LANES = 128
TILE = 256


def kernel(
    dims, h_hbm, w_hbm, t_hbm, rw_hbm, out_ref, loss_ref,
    h_ref, t_ref, rw_ref, in_sem, w_ref, w_sem, hid, pieces, tall, wide_rows, zg_s, zg_r, xg_s, xg_r, cg_s, cg_r,
    logits, soft, tcol, stat, srow, s_cx, s_z, s_loss, sc_s, sc_r, sz_s, sz_r, sl_s, sl_r,
    t_out, t_in, t_own, tx_in, tc_s, tc_r, tx_s, tx_r,
    c_out, c_in, rc_s, rc_r, whole_ref, x_out, x_in, x_own, rx_s, rx_r,
    acc, z_out, z_in, rz_s, rz_r, flat,
):
    nzlo, nx = dims
    nz = 2 * nzlo
    rb, wide = h_ref.shape
    quarters = wide // LANES
    rows = nzlo * nx * rb
    xrows = nzlo * rb
    step = 48
    vocab = w_ref.shape[1]
    per_x = xrows // step
    zlo, x = lax.axis_index("zlo"), lax.axis_index("x")
    zhi, core = lax.axis_index("zhi"), lax.axis_index("core")
    z = zhi * nzlo + zlo
    other = 1 - core
    pairs = wide // TILE

    def at_z(k):
        k = lax.rem(k + nz, nz)
        return {"zhi": k // nzlo, "zlo": lax.rem(k, nzlo)}

    def at_x(k):
        return {"x": lax.rem(k, nx)}

    at_core = {"core": other}

    def remote(src, dst, send, recv, where):
        return pltpu.make_async_remote_copy(
            src_ref=src, dst_ref=dst, send_sem=send, recv_sem=recv, device_id=where, device_id_type=MESH
        )

    def rows_of(k, size):
        return pl.ds(pl.multiple_of(k * size, size), size)

    barrier = pltpu.get_barrier_semaphore()
    partners = [at_z(z + d) for d in range(1, nz)] + [at_x(x + d) for d in range(1, nx)] + [at_core]
    for where in partners:
        pl.semaphore_signal(barrier, inc=1, device_id=where, device_id_type=MESH)
    small = [
        pltpu.make_async_copy(t_hbm, t_ref, in_sem.at[0]),
        pltpu.make_async_copy(rw_hbm, rw_ref, in_sem.at[1]),
        pltpu.make_async_copy(h_hbm, h_ref, in_sem.at[2]),
    ]
    for copy in small:
        copy.start()
    w_copy = pltpu.make_async_copy(w_hbm, w_ref, w_sem)
    w_copy.start()

    srow[...] = jnp.zeros_like(srow)
    for copy in small:
        copy.wait()
    srow[0:1, 0:rows] = t_ref[...].astype(F32).reshape(1, rows)
    srow[1:2, 0:rows] = rw_ref[...].reshape(1, rows)
    stat[...] = jnp.transpose(srow[...], (1, 0))
    for i in range(nx):
        for j in range(nzlo):
            to, of = (i * nzlo + j) * rb, (j * nx + i) * rb
            tcol[to : to + rb, :] = stat[of : of + rb, :]

    for j in range(quarters):
        tall[0, j * rb : (j + 1) * rb, :] = h_ref[:, j * LANES : (j + 1) * LANES].astype(F32)
    pieces[z] = tall[0].astype(BF16)

    offset = ((zlo * nx + x) * 4 + zhi * 2 + core) * vocab
    lane = lax.broadcasted_iota(jnp.int32, (step, LANES), 1)
    column = lax.broadcasted_iota(jnp.int32, (step, vocab), 1)

    def is_target(span):
        wanted = tcol[span, 0:1].astype(jnp.int32) - offset
        return column == wanted

    @pl.loop(0, rows // step)
    def _(r):
        span = rows_of(r, step)
        soft[span, :] = jnp.where(is_target(span), 1.0, 0.0).astype(BF16)

    def product(half, who, pair):
        first = (half * 2 + who) * wide + pair * TILE
        part = w_ref[pl.ds(pl.multiple_of(first, TILE), TILE), :]
        return lax.dot_general(soft[...], part, (((1,), (1,)), ((), ())), preferred_element_type=F32)

    def tile(pair):
        return rows_of(pair, TILE)

    def padded(r):
        first = (r // per_x) * LANES + lax.rem(r, per_x) * step
        return pl.ds(pl.multiple_of(first, 16), step)

    pl.semaphore_wait(barrier, len(partners))

    def gather_z(d):
        k = lax.rem(z + d + nz, nz)
        return remote(pieces.at[z], pieces.at[z], zg_s.at[k], zg_r.at[z], at_z(z + d))

    for d in range(1, nz // 2):
        gather_z(d).start()
        gather_z(-d).start()
    gather_z(nz // 2).start()

    w_copy.wait()

    @pl.loop(0, 2 * pairs)
    def _(n):
        half, pair = n // pairs, lax.rem(n, pairs)
        t_out[half, :, tile(pair)] = product(half, other, pair).astype(BF16)
        t_own[half, :, tile(pair)] = product(half, core, pair).astype(BF16)

    def t_core(half):
        return remote(t_out.at[half], t_in.at[half], tc_s.at[half], tc_r.at[half], at_core)

    t_core(0).start()
    t_core(1).start()

    size = min(4, nzlo)
    groups = nz // size
    grows = size * rb
    per_half = groups // 2

    def place(g, chunk_x):
        first = chunk_x * xrows + lax.rem(g, per_half) * grows
        return hid.at[(g // per_half) * 2 + core, pl.ds(pl.multiple_of(first, grows), grows), :]

    def over_x(g, d):
        return remote(place(g, x), place(g, x), xg_s.at[g, d - 1], xg_r.at[g, d - 1], at_x(x + d))

    def over_core(g, d):
        whose = lax.rem(x + d, nx)
        return remote(place(g, whose), place(g, whose), cg_s.at[g, d], cg_r.at[g, d], at_core)

    def pass_to_core(g):
        for d in range(1, nx):
            over_x(g, nx - d).wait_recv()
            over_core(g, d).start()

    def take_group(g):
        for i in range(size):
            k = g * size + i

            @pl.when(k != z)
            def _():
                remote(pieces.at[k], pieces.at[k], zg_s.at[k], zg_r.at[k], at_core).wait_recv()

            tall[i] = pieces[k].astype(F32)
            for j in range(quarters):
                wide_rows[i * rb : (i + 1) * rb, j * LANES : (j + 1) * LANES] = tall[i, j * rb : (j + 1) * rb, :]
        first = x * xrows + lax.rem(g, per_half) * grows
        hid[(g // per_half) * 2 + core, pl.ds(pl.multiple_of(first, grows), grows), :] = wide_rows[...].astype(BF16)
        for d in range(1, nx):
            over_x(g, d).start()
        over_core(g, 0).start()

    def in_turn(i):
        if groups == 2:
            return lax.rem(z // size + i, groups)
        shift = jnp.where(i == 2, 3, jnp.where(i == 3, 2, i))
        return lax.rem(z // size + shift, groups)

    @pl.loop(0, groups)
    def _(i):
        take_group(in_turn(i))

        @pl.when(i > 0)
        def _():
            pass_to_core(in_turn(i - 1))

    def t_over_x(half, d):
        q = lax.rem(x + d, nx)
        return remote(
            t_own.at[half, rows_of(q, xrows), :], tx_in.at[d - 1, half], tx_s.at[half, d - 1], tx_r.at[half, d - 1], at_x(q)
        )

    for half in range(2):
        t_core(half).wait_recv()

        @pl.loop(0, rows // step)
        def _(r):
            span = rows_of(r, step)
            t_own[half, span, :] = (t_own[half, span, :].astype(F32) + t_in[half, span, :].astype(F32)).astype(BF16)

    pass_to_core(in_turn(groups - 1))

    for half in range(2):
        for d in range(1, nx):
            t_over_x(half, d).start()

    @pl.loop(0, groups)
    def _(g):
        for d in range(nx):
            over_core(g, d).wait_recv()

    def all_rows():
        return jnp.concatenate([hid[k] for k in range(4)], axis=1)

    @pl.loop(0, vocab // TILE)
    def _(n):
        cols = tile(n)
        logits[:, cols] = jnp.dot(all_rows(), w_ref[:, cols], preferred_element_type=F32)

    if vocab % TILE:
        logits[:, vocab // TILE * TILE :] = jnp.dot(
            all_rows(), w_ref[:, vocab // TILE * TILE :], preferred_element_type=F32
        )

    @pl.loop(0, rows // step)
    def _(r):
        span = rows_of(r, step)
        part = logits[span, :]
        top = jnp.max(part, axis=1, keepdims=True)
        shifted = jnp.exp(part - top)
        soft[span, :] = shifted.astype(BF16)
        summed = jnp.sum(shifted, axis=1, keepdims=True)
        label = jnp.sum(jnp.where(is_target(span), part, 0.0), axis=1, keepdims=True)
        stat[padded(r), :] = jnp.where(lane == 0, top, jnp.where(lane == 1, summed, jnp.where(lane == 2, label, 0.0)))

    def joined(slots):
        tops = slots[:, 0:1, :]
        top = jnp.max(tops, axis=0)
        summed = jnp.sum(slots[:, 1:2, :] * jnp.exp(tops - top[None]), axis=0)
        return top, summed, jnp.sum(slots[:, 2:3, :], axis=0)

    flipped = jnp.transpose(stat[...], (1, 0))
    here = x * 2 + core
    s_cx[here] = flipped[0:4, :]

    def stats_cx(n):
        d, c = n // 2, n % 2
        return remote(
            s_cx.at[here], s_cx.at[here], sc_s.at[n], sc_r.at[n], {"x": lax.rem(x + d, nx), "core": lax.rem(core + c, 2)}
        )

    for n in range(1, 2 * nx):
        stats_cx(n).start()

    def to_core(half, pair):
        n = half * pairs + pair
        part = c_out.at[half, :, tile(pair)]
        return remote(part, c_in.at[half, :, tile(pair)], rc_s.at[n], rc_r.at[n], at_core)

    def for_partner(half):
        @pl.loop(0, pairs)
        def _(pair):
            c_out[half, :, tile(pair)] = product(half, other, pair).astype(BF16)
            to_core(half, pair).start()

    for_partner(0)
    stats_cx(1).wait()
    mine = s_cx[here, 0:1, :]
    theirs = s_cx[x * 2 + other, 0:1, :]
    core_top = jnp.maximum(mine, theirs)
    srow[0:1, :] = jnp.exp(mine - core_top)
    srow[1:2, :] = jnp.exp(theirs - core_top)
    stat[...] = jnp.transpose(srow[...], (1, 0))

    def to_x(half, pair, d):
        q = lax.rem(x + d, nx)
        n = half * pairs + pair
        return remote(
            x_out.at[half, rows_of(q, xrows), tile(pair)], x_in.at[d - 1, half, :, tile(pair)],
            rx_s.at[n, d - 1], rx_r.at[n, d - 1], at_x(q),
        )

    def for_self(half, pair):
        whole_ref[...] = product(half, core, pair)
        to_core(half, pair).wait_recv()

        @pl.loop(0, rows // step)
        def _(r):
            span = rows_of(r, step)
            got = c_in[half, span, tile(pair)].astype(F32)
            whole = whole_ref[span, :] * stat[padded(r), 0:1] + got * stat[padded(r), 1:2]
            whole_ref[span, :] = whole
            x_out[half, span, tile(pair)] = whole.astype(BF16)

        x_own[half, :, tile(pair)] = whole_ref[rows_of(x, xrows), :]
        for d in range(1, nx):
            to_x(half, pair, d).start()

    @pl.loop(0, pairs)
    def _(pair):
        for_self(0, pair)

    for_partner(1)

    @pl.loop(0, pairs)
    def _(pair):
        for_self(1, pair)

    for n in range(2, 2 * nx):
        stats_cx(n).wait()
    all_top, all_sum, all_label = joined(s_cx[...])
    srow[0:1, :] = all_top
    srow[1:2, :] = all_sum
    srow[2:3, :] = all_label
    for d in range(nx):
        there = lax.rem(x + nx - d, nx) * 2
        top = jnp.maximum(s_cx[there, 0:1, :], s_cx[there + 1, 0:1, :])
        srow[4 + d : 5 + d, :] = jnp.exp(top - all_top)
    own_lanes = pl.ds(pl.multiple_of(x * LANES, LANES), LANES)
    s_z[z] = srow[0:4, own_lanes]

    def stats_z(d):
        return remote(s_z.at[z], s_z.at[z], sz_s.at[d], sz_r.at[d], at_z(z + d))

    @pl.loop(1, nz)
    def _(d):
        stats_z(d).start()

    flat[...] = jnp.transpose(srow[:, own_lanes], (1, 0))
    own_rows = rows_of(x, xrows)

    @pl.loop(0, 2)
    def _(half):
        for d in range(1, nx):
            for pair in range(pairs):
                to_x(half, pair, d).wait_recv()
        whole = x_own[half] * flat[0:xrows, 4:5]
        for d in range(1, nx):
            whole += x_in[d - 1, half].astype(F32) * flat[0:xrows, 4 + d : 5 + d]
        acc[half] = whole

    @pl.loop(1, nz)
    def _(d):
        stats_z(d).wait()

    top, summed, label = joined(s_z[...])
    srow[0:1, 0:LANES] = jnp.exp(s_z[z, 0:1, :] - top) / summed
    flat[...] = jnp.transpose(srow[:, 0:LANES], (1, 0))
    s_loss[x] = jnp.broadcast_to(jnp.log(summed) + top - label, (8, LANES))

    def losses(d):
        return remote(s_loss.at[x], s_loss.at[x], sl_s.at[d - 1], sl_r.at[d - 1], at_x(x + d))

    def to_z(k):
        return remote(z_out.at[k], z_in.at[z], rz_s.at[k], rz_r.at[z], at_z(k))

    @pl.loop(0, 2)
    def _(half):
        weight = tcol[own_rows, 1:2]
        hit = t_own[half, own_rows, :].astype(F32)
        for d in range(1, nx):
            t_over_x(half, d).wait_recv()
            hit += tx_in[d - 1, half].astype(F32)
        acc[half] = acc[half] * (weight * flat[0:xrows, 0:1]) - weight * hit
        for low in range(nzlo):
            slot = low % 4
            for j in range(quarters):
                tall[slot, j * rb : (j + 1) * rb, :] = acc[half, low * rb : (low + 1) * rb, j * LANES : (j + 1) * LANES]
            k = half * nzlo + low

            @pl.when(k == z)
            def _():
                tall[4] = tall[slot]

            @pl.when(k != z)
            def _():
                z_out[k] = tall[slot].astype(BF16)
                to_z(k).start()

    for d in range(1, nx):
        losses(d).start()
    for d in range(1, nx):
        losses(d).wait()
    for i in range(nx):
        srow[0:1, i * LANES : (i + 1) * LANES] = s_loss[i, 0:1, :]
    stat[...] = jnp.transpose(srow[...], (1, 0))
    for i in range(nx):
        for j in range(nzlo):
            of, to = i * LANES + j * rb, (j * nx + i) * rb
            logits[to : to + rb, 0:LANES] = stat[of : of + rb, :]
    loss_ref[...] = jnp.transpose(logits[:, 0:LANES], (1, 0))[0:1, :].reshape(rows)

    @pl.loop(0, nz)
    def _(k):
        @pl.when(k != z)
        def _():
            remote(z_in.at[k], z_in.at[k], rz_s.at[k], rz_r.at[k], at_core).wait_recv()
            tall[4] += z_in[k].astype(F32)

    for j in range(quarters):
        out_ref[:, j * LANES : (j + 1) * LANES] = tall[4, j * rb : (j + 1) * rb, :].astype(BF16)

    @pl.loop(1, nz)
    def _(d):
        gather_z(d).wait_send()
        to_z(lax.rem(z + d, nz)).wait_send()

    @pl.loop(0, groups)
    def _(g):
        over_core(g, 0).wait_send()
        for d in range(1, nx):
            over_core(g, d).wait_send()
            over_x(g, d).wait_send()

    @pl.loop(0, 2)
    def _(half):
        t_core(half).wait_send()
        for d in range(1, nx):
            t_over_x(half, d).wait_send()
        for pair in range(pairs):
            to_core(half, pair).wait_send()
            for d in range(1, nx):
                to_x(half, pair, d).wait_send()


def per_device(dims, hidden, weight, targets, row_weight):
    nzlo, nx = dims
    nz = 2 * nzlo
    rb, wide = hidden.shape
    depth, vocab = weight.shape
    rows = targets.shape[0]
    xrows = nzlo * rb
    size = min(4, nzlo)
    groups = nz // size
    tallness = rb * wide // LANES
    pairs = wide // TILE
    vmem, dma = pltpu.VMEM, pltpu.SemaphoreType.DMA
    spec = pl.BlockSpec(memory_space=pltpu.VMEM)
    halves = vmem((2, rows, wide), BF16)
    scratch = [
        vmem((rb, wide), BF16), vmem((rows,), jnp.int32), vmem((rows,), F32), dma((3,)),
        vmem((depth, vocab), BF16), dma(()),
        vmem((4, rows, wide), BF16), vmem((nz, tallness, LANES), BF16), vmem((5, tallness, LANES), F32),
        vmem((size * rb, wide), F32),
        dma((nz,)), dma((nz,)), dma((groups, nx - 1)), dma((groups, nx - 1)), dma((groups, nx)), dma((groups, nx)),
        vmem((rows, vocab), F32), vmem((rows, vocab), BF16), vmem((rows, LANES), F32),
        vmem((nx * LANES, LANES), F32), vmem((LANES, nx * LANES), F32),
        vmem((2 * nx, 4, nx * LANES), F32), vmem((nz, 4, LANES), F32), vmem((nx, 8, LANES), F32),
        dma((2 * nx,)), dma((2 * nx,)), dma((nz,)), dma((nz,)), dma((nx - 1,)), dma((nx - 1,)),
        halves, halves, halves, vmem((nx - 1, 2, xrows, wide), BF16),
        dma((2,)), dma((2,)), dma((2, nx - 1)), dma((2, nx - 1)),
        halves, halves, dma((2 * pairs,)), dma((2 * pairs,)), vmem((rows, TILE), F32),
        halves, vmem((nx - 1, 2, xrows, wide), BF16), vmem((2, xrows, wide), F32),
        dma((2 * pairs, nx - 1)), dma((2 * pairs, nx - 1)),
        vmem((2, xrows, wide), F32), vmem((nz, tallness, LANES), BF16), vmem((nz, tallness, LANES), BF16),
        dma((nz,)), dma((nz,)), vmem((LANES, LANES), F32),
    ]
    return pl.pallas_call(
        functools.partial(kernel, dims),
        out_shape=(
            jax.ShapeDtypeStruct((rb, wide), BF16),
            jax.ShapeDtypeStruct((rows,), F32),
        ),
        in_specs=[pl.BlockSpec(memory_space=pl.ANY)] * 4,
        out_specs=(spec, spec),
        scratch_shapes=scratch,
        compiler_params=pltpu.CompilerParams(collective_id=0, has_side_effects=True),
    )(hidden, weight, targets, row_weight)


def on_mesh(split):
    dims = (split.shape["zlo"], split.shape["x"])
    tensor, pipe = ("zhi", "core"), ("zlo", "x")
    in_specs = (P(("dp", *pipe), tensor), P(None, (*pipe, *tensor)), P("dp"), P("dp"))
    out_specs = (P(("dp", *pipe), tensor), P("dp"))
    return jax.shard_map(
        functools.partial(per_device, dims), mesh=split, in_specs=in_specs, out_specs=out_specs, check_vma=False
    )


def solution(mesh):
    return on_mesh(Mesh(mesh.devices.reshape(mesh.shape["dp"], 8, 4, 2, 2), AXES))
```

```python
import functools

import jax
import jax.numpy as jnp
from jax import lax
from jax.experimental import pallas as pl
from jax.experimental.pallas import tpu as pltpu
from jax.sharding import Mesh
from jax.sharding import PartitionSpec as P

AXES = ("dp", "zlo", "x", "zhi", "core")
MESH = pl.DeviceIdType.MESH
F32 = jnp.float32
BF16 = jnp.bfloat16
LANES = 128
TILE = 256


def kernel(
    dims, h_hbm, w_hbm, t_hbm, rw_hbm, out_ref, loss_ref,
    h_ref, t_ref, rw_ref, in_sem, w_ref, w_sem, hid, pieces, tall, wide_rows, zg_s, zg_r, xg_s, xg_r, cg_s, cg_r,
    logits, soft, tcol, stat, srow, s_cx, s_z, s_loss, sc_s, sc_r, sz_s, sz_r, sl_s, sl_r,
    t_out, t_in, t_own, tx_in, tc_s, tc_r, tx_s, tx_r,
    c_out, c_in, rc_s, rc_r, whole_ref, x_out, x_in, x_own, rx_s, rx_r,
    acc, z_out, z_in, rz_s, rz_r, flat, factor,
):
    nzlo, nx = dims
    nz = 2 * nzlo
    rb, wide = h_ref.shape
    quarters = wide // LANES
    rows = nzlo * nx * rb
    xrows = nzlo * rb
    step = 48
    vocab = w_ref.shape[1]
    per_x = xrows // step
    zlo, x = lax.axis_index("zlo"), lax.axis_index("x")
    zhi, core = lax.axis_index("zhi"), lax.axis_index("core")
    z = zhi * nzlo + zlo
    other = 1 - core
    pairs = wide // TILE

    def at_z(k):
        k = lax.rem(k + nz, nz)
        return {"zhi": k // nzlo, "zlo": lax.rem(k, nzlo)}

    def at_x(k):
        return {"x": lax.rem(k, nx)}

    at_core = {"core": other}

    def remote(src, dst, send, recv, where):
        return pltpu.make_async_remote_copy(
            src_ref=src, dst_ref=dst, send_sem=send, recv_sem=recv, device_id=where, device_id_type=MESH
        )

    def rows_of(k, size):
        return pl.ds(pl.multiple_of(k * size, size), size)

    barrier = pltpu.get_barrier_semaphore()
    reach = nz // 4
    partners = [at_z(z + d) for d in range(-reach, reach + 1) if d] + [at_x(x + d) for d in range(1, nx)] + [at_core]
    for where in partners:
        pl.semaphore_signal(barrier, inc=1, device_id=where, device_id_type=MESH)
    small = [
        pltpu.make_async_copy(t_hbm, t_ref, in_sem.at[0]),
        pltpu.make_async_copy(rw_hbm, rw_ref, in_sem.at[1]),
        pltpu.make_async_copy(h_hbm, h_ref, in_sem.at[2]),
    ]
    for copy in small:
        copy.start()
    w_copy = pltpu.make_async_copy(w_hbm, w_ref, w_sem)
    w_copy.start()

    srow[...] = jnp.zeros_like(srow)
    for copy in small:
        copy.wait()
    srow[0:1, 0:rows] = t_ref[...].astype(F32).reshape(1, rows)
    srow[1:2, 0:rows] = rw_ref[...].reshape(1, rows)
    stat[...] = jnp.transpose(srow[...], (1, 0))
    for i in range(nx):
        for j in range(nzlo):
            to, of = (i * nzlo + j) * rb, (j * nx + i) * rb
            tcol[to : to + rb, :] = stat[of : of + rb, :]

    for j in range(quarters):
        tall[0, j * rb : (j + 1) * rb, :] = h_ref[:, j * LANES : (j + 1) * LANES].astype(F32)
    pieces[z] = tall[0].astype(BF16)

    offset = ((zlo * nx + x) * 4 + zhi * 2 + core) * vocab
    lane = lax.broadcasted_iota(jnp.int32, (step, LANES), 1)
    column = lax.broadcasted_iota(jnp.int32, (step, vocab), 1)

    def is_target(span):
        wanted = tcol[span, 0:1].astype(jnp.int32) - offset
        return column == wanted

    @pl.loop(0, rows // step)
    def _(r):
        span = rows_of(r, step)
        soft[span, :] = jnp.where(is_target(span), 1.0, 0.0).astype(BF16)

    def product(half, who, pair):
        first = (half * 2 + who) * wide + pair * TILE
        part = w_ref[pl.ds(pl.multiple_of(first, TILE), TILE), :]
        return lax.dot_general(soft[...], part, (((1,), (1,)), ((), ())), preferred_element_type=F32)

    def tile(pair):
        return rows_of(pair, TILE)

    def padded(r):
        first = (r // per_x) * LANES + lax.rem(r, per_x) * step
        return pl.ds(pl.multiple_of(first, 16), step)

    pl.semaphore_wait(barrier, len(partners))

    def gather_z(whose, d, n):
        k = lax.rem(whose + nz, nz)
        return remote(pieces.at[k], pieces.at[k], zg_s.at[n], zg_r.at[k], at_z(z + d))

    direct = [gather_z(z, sign * d, 2 * (reach - d) + (sign > 0)) for d in range(reach, 0, -1) for sign in (-1, 1)]
    onward = [gather_z(z - reach, d, 2 * reach + d - 1) for d in range(reach - 1, 0, -1)]
    backward = [gather_z(z + reach, -d, 3 * reach + d - 2) for d in range(reach, 0, -1)]
    for copy in direct:
        copy.start()

    w_copy.wait()

    @pl.loop(0, 2 * pairs)
    def _(n):
        half, pair = n // pairs, lax.rem(n, pairs)
        t_out[half, :, tile(pair)] = product(half, other, pair).astype(BF16)
        t_own[half, :, tile(pair)] = product(half, core, pair).astype(BF16)

    def t_core(half):
        return remote(t_out.at[half], t_in.at[half], tc_s.at[half], tc_r.at[half], at_core)

    t_core(0).start()
    t_core(1).start()

    size = min(4, nzlo)
    groups = nz // size
    grows = size * rb
    per_half = groups // 2

    def place(g, chunk_x):
        first = chunk_x * xrows + lax.rem(g, per_half) * grows
        return hid.at[(g // per_half) * 2 + core, pl.ds(pl.multiple_of(first, grows), grows), :]

    def over_x(g, d):
        return remote(place(g, x), place(g, x), xg_s.at[g, d - 1], xg_r.at[g, d - 1], at_x(x + d))

    def over_core(g, d):
        whose = lax.rem(x + d, nx)
        return remote(place(g, whose), place(g, whose), cg_s.at[g, d], cg_r.at[g, d], at_core)

    def pass_to_core(g):
        for d in range(1, nx):
            over_x(g, nx - d).wait_recv()
            over_core(g, d).start()

    def take_group(g):
        for i in range(size):
            k = g * size + i

            away = lax.rem(k - z + nz, nz)

            @pl.when((away != 0) & (away != reach) & (away != nz - reach))
            def _():
                remote(pieces.at[k], pieces.at[k], zg_s.at[0], zg_r.at[k], at_core).wait_recv()

            tall[i] = pieces[k].astype(F32)
            for j in range(quarters):
                wide_rows[i * rb : (i + 1) * rb, j * LANES : (j + 1) * LANES] = tall[i, j * rb : (j + 1) * rb, :]
        first = x * xrows + lax.rem(g, per_half) * grows
        hid[(g // per_half) * 2 + core, pl.ds(pl.multiple_of(first, grows), grows), :] = wide_rows[...].astype(BF16)
        for d in range(1, nx):
            over_x(g, d).start()
        over_core(g, 0).start()

    def in_turn(i):
        half = lax.rem(zhi + i // per_half, 2)
        return half * per_half + lax.rem(zlo // size + i, per_half)

    for source, copies in ((z - reach, onward), (z + reach, backward)):
        k = lax.rem(source + nz, nz)
        remote(pieces.at[k], pieces.at[k], zg_s.at[0], zg_r.at[k], at_core).wait_recv()
        for copy in copies:
            copy.start()

    @pl.loop(0, groups)
    def _(i):
        take_group(in_turn(i))

        @pl.when(i > 0)
        def _():
            pass_to_core(in_turn(i - 1))

    def t_over_x(half, d):
        q = lax.rem(x + d, nx)
        return remote(
            t_own.at[half, rows_of(q, xrows), :], tx_in.at[d - 1, half], tx_s.at[half, d - 1], tx_r.at[half, d - 1], at_x(q)
        )

    for half in range(2):
        t_core(half).wait_recv()

        @pl.loop(0, rows // step)
        def _(r):
            span = rows_of(r, step)
            t_own[half, span, :] = (t_own[half, span, :].astype(F32) + t_in[half, span, :].astype(F32)).astype(BF16)

    def arrived(half):
        @pl.loop(0, per_half)
        def _(g):
            for d in range(nx):
                over_core(half * per_half + g, d).wait_recv()

    def half_rows(half):
        return jnp.concatenate([hid[2 * half], hid[2 * half + 1]], axis=1)

    def depth(half):
        return pl.ds(pl.multiple_of(half * 2 * wide, 2 * wide), 2 * wide)

    last = vocab // TILE * TILE
    arrived(zhi)

    @pl.loop(0, vocab // TILE)
    def _(n):
        cols = tile(n)
        logits[:, cols] = jnp.dot(half_rows(zhi), w_ref[depth(zhi), cols], preferred_element_type=F32)

    if vocab % TILE:
        logits[:, last:] = jnp.dot(half_rows(zhi), w_ref[depth(zhi), last:], preferred_element_type=F32)

    pass_to_core(in_turn(groups - 1))

    for half in range(2):
        for d in range(1, nx):
            t_over_x(half, d).start()

    far = 1 - zhi
    arrived(far)

    @pl.loop(0, vocab // TILE)
    def _(n):
        cols = tile(n)
        logits[:, cols] += jnp.dot(half_rows(far), w_ref[depth(far), cols], preferred_element_type=F32)

    if vocab % TILE:
        logits[:, last:] += jnp.dot(half_rows(far), w_ref[depth(far), last:], preferred_element_type=F32)

    @pl.loop(0, rows // step)
    def _(r):
        span = rows_of(r, step)
        part = logits[span, :]
        top = jnp.max(part, axis=1, keepdims=True)
        shifted = jnp.exp(part - top)
        soft[span, :] = shifted.astype(BF16)
        summed = jnp.sum(shifted, axis=1, keepdims=True)
        label = jnp.sum(jnp.where(is_target(span), part, 0.0), axis=1, keepdims=True)
        stat[padded(r), :] = jnp.where(lane == 0, top, jnp.where(lane == 1, summed, jnp.where(lane == 2, label, 0.0)))

    def joined(slots):
        tops = slots[:, 0:1, :]
        top = jnp.max(tops, axis=0)
        summed = jnp.sum(slots[:, 1:2, :] * jnp.exp(tops - top[None]), axis=0)
        return top, summed, jnp.sum(slots[:, 2:3, :], axis=0)

    flipped = jnp.transpose(stat[...], (1, 0))
    here = x * 2 + core
    s_cx[here] = flipped[0:4, :]

    def stats_cx(n):
        d, c = n // 2, n % 2
        return remote(
            s_cx.at[here], s_cx.at[here], sc_s.at[n], sc_r.at[n], {"x": lax.rem(x + d, nx), "core": lax.rem(core + c, 2)}
        )

    for n in range(1, 2 * nx):
        stats_cx(n).start()

    def to_core(half, pair):
        n = half * pairs + pair
        part = c_out.at[half, :, tile(pair)]
        return remote(part, c_in.at[half, :, tile(pair)], rc_s.at[n], rc_r.at[n], at_core)

    def for_partner(half):
        @pl.loop(0, pairs)
        def _(pair):
            c_out[half, :, tile(pair)] = product(half, other, pair).astype(BF16)
            to_core(half, pair).start()

    for_partner(0)
    stats_cx(1).wait()
    mine = s_cx[here, 0:1, :]
    theirs = s_cx[x * 2 + other, 0:1, :]
    core_top = jnp.maximum(mine, theirs)
    for k, own in enumerate((mine, theirs)):
        srow[...] = jnp.broadcast_to(jnp.exp(own - core_top), srow.shape)
        stat[...] = jnp.transpose(srow[...], (1, 0))
        for i in range(nx):
            factor[k, i * xrows : (i + 1) * xrows, :] = stat[i * LANES : i * LANES + xrows, :]

    def to_x(half, pair, d):
        q = lax.rem(x + d, nx)
        n = half * pairs + pair
        return remote(
            x_out.at[half, rows_of(q, xrows), tile(pair)], x_in.at[d - 1, half, :, tile(pair)],
            rx_s.at[n, d - 1], rx_r.at[n, d - 1], at_x(q),
        )

    def for_self(half, pair):
        whole_ref[...] = product(half, core, pair)
        to_core(half, pair).wait_recv()

        for k in range(TILE // LANES):
            lanes = pl.ds(pl.multiple_of(pair * TILE + k * LANES, LANES), LANES)
            whole = whole_ref[:, k * LANES : (k + 1) * LANES] * factor[0] + c_in[half, :, lanes].astype(F32) * factor[1]
            whole_ref[:, k * LANES : (k + 1) * LANES] = whole
            x_out[half, :, lanes] = whole.astype(BF16)

        x_own[half, :, tile(pair)] = whole_ref[rows_of(x, xrows), :]
        for d in range(1, nx):
            to_x(half, pair, d).start()

    @pl.loop(0, pairs)
    def _(pair):
        for_self(0, pair)

    for_partner(1)

    for n in range(2, 2 * nx):
        stats_cx(n).wait()
    all_top, all_sum, all_label = joined(s_cx[...])
    srow[0:1, :] = all_top
    srow[1:2, :] = all_sum
    srow[2:3, :] = all_label
    for d in range(nx):
        there = lax.rem(x + nx - d, nx) * 2
        top = jnp.maximum(s_cx[there, 0:1, :], s_cx[there + 1, 0:1, :])
        srow[4 + d : 5 + d, :] = jnp.exp(top - all_top)
    own_lanes = pl.ds(pl.multiple_of(x * LANES, LANES), LANES)
    s_z[z] = srow[0:4, own_lanes]

    def stats_z(d):
        return remote(s_z.at[z], s_z.at[z], sz_s.at[d], sz_r.at[d], at_z(z + d))

    @pl.loop(1, nz)
    def _(d):
        stats_z(d).start()

    flat[...] = jnp.transpose(srow[:, own_lanes], (1, 0))
    own_rows = rows_of(x, xrows)

    @pl.loop(0, pairs)
    def _(pair):
        for_self(1, pair)

    @pl.loop(0, 2)
    def _(half):
        for d in range(1, nx):
            for pair in range(pairs):
                to_x(half, pair, d).wait_recv()
        whole = x_own[half] * flat[0:xrows, 4:5]
        for d in range(1, nx):
            whole += x_in[d - 1, half].astype(F32) * flat[0:xrows, 4 + d : 5 + d]
        acc[half] = whole

    @pl.loop(1, nz)
    def _(d):
        stats_z(d).wait()

    top, summed, label = joined(s_z[...])
    srow[0:1, 0:LANES] = jnp.exp(s_z[z, 0:1, :] - top) / summed
    flat[...] = jnp.transpose(srow[:, 0:LANES], (1, 0))
    s_loss[x] = jnp.broadcast_to(jnp.log(summed) + top - label, (8, LANES))

    def losses(d):
        return remote(s_loss.at[x], s_loss.at[x], sl_s.at[d - 1], sl_r.at[d - 1], at_x(x + d))

    def to_z(k):
        return remote(z_out.at[k], z_in.at[z], rz_s.at[k], rz_r.at[z], at_z(k))

    @pl.loop(0, 2)
    def _(half):
        weight = tcol[own_rows, 1:2]
        hit = t_own[half, own_rows, :].astype(F32)
        for d in range(1, nx):
            t_over_x(half, d).wait_recv()
            hit += tx_in[d - 1, half].astype(F32)
        acc[half] = acc[half] * (weight * flat[0:xrows, 0:1]) - weight * hit
        for low in range(nzlo):
            slot = low % 4
            for j in range(quarters):
                tall[slot, j * rb : (j + 1) * rb, :] = acc[half, low * rb : (low + 1) * rb, j * LANES : (j + 1) * LANES]
            k = half * nzlo + low

            @pl.when(k == z)
            def _():
                tall[4] = tall[slot]

            z_out[k] = tall[slot].astype(BF16)

    to_z(lax.rem(z + nz // 2, nz)).start()
    for d in range(nz // 2 - 1, 0, -1):
        to_z(lax.rem(z + d, nz)).start()
        to_z(lax.rem(z + nz - d, nz)).start()

    for d in range(1, nx):
        losses(d).start()
    for d in range(1, nx):
        losses(d).wait()
    for i in range(nx):
        srow[0:1, i * LANES : (i + 1) * LANES] = s_loss[i, 0:1, :]
    stat[...] = jnp.transpose(srow[...], (1, 0))
    for i in range(nx):
        for j in range(nzlo):
            of, to = i * LANES + j * rb, (j * nx + i) * rb
            logits[to : to + rb, 0:LANES] = stat[of : of + rb, :]
    loss_ref[...] = jnp.transpose(logits[:, 0:LANES], (1, 0))[0:1, :].reshape(rows)

    @pl.loop(0, nz)
    def _(k):
        @pl.when(k != z)
        def _():
            remote(z_in.at[k], z_in.at[k], rz_s.at[k], rz_r.at[k], at_core).wait_recv()
            tall[4] += z_in[k].astype(F32)

    for j in range(quarters):
        out_ref[:, j * LANES : (j + 1) * LANES] = tall[4, j * rb : (j + 1) * rb, :].astype(BF16)

    @pl.loop(1, nz)
    def _(d):
        to_z(lax.rem(z + d, nz)).wait_send()

    for copy in direct + onward + backward:
        copy.wait_send()

    @pl.loop(0, groups)
    def _(g):
        over_core(g, 0).wait_send()
        for d in range(1, nx):
            over_core(g, d).wait_send()
            over_x(g, d).wait_send()

    @pl.loop(0, 2)
    def _(half):
        t_core(half).wait_send()
        for d in range(1, nx):
            t_over_x(half, d).wait_send()
        for pair in range(pairs):
            to_core(half, pair).wait_send()
            for d in range(1, nx):
                to_x(half, pair, d).wait_send()


def per_device(dims, hidden, weight, targets, row_weight):
    nzlo, nx = dims
    nz = 2 * nzlo
    rb, wide = hidden.shape
    depth, vocab = weight.shape
    rows = targets.shape[0]
    xrows = nzlo * rb
    size = min(4, nzlo)
    groups = nz // size
    tallness = rb * wide // LANES
    pairs = wide // TILE
    vmem, dma = pltpu.VMEM, pltpu.SemaphoreType.DMA
    spec = pl.BlockSpec(memory_space=pltpu.VMEM)
    halves = vmem((2, rows, wide), BF16)
    scratch = [
        vmem((rb, wide), BF16), vmem((rows,), jnp.int32), vmem((rows,), F32), dma((3,)),
        vmem((depth, vocab), BF16), dma(()),
        vmem((4, rows, wide), BF16), vmem((nz, tallness, LANES), BF16), vmem((5, tallness, LANES), F32),
        vmem((size * rb, wide), F32),
        dma((nz,)), dma((nz,)), dma((groups, nx - 1)), dma((groups, nx - 1)), dma((groups, nx)), dma((groups, nx)),
        vmem((rows, vocab), F32), vmem((rows, vocab), BF16), vmem((rows, LANES), F32),
        vmem((nx * LANES, LANES), F32), vmem((LANES, nx * LANES), F32),
        vmem((2 * nx, 4, nx * LANES), F32), vmem((nz, 4, LANES), F32), vmem((nx, 8, LANES), F32),
        dma((2 * nx,)), dma((2 * nx,)), dma((nz,)), dma((nz,)), dma((nx - 1,)), dma((nx - 1,)),
        halves, halves, halves, vmem((nx - 1, 2, xrows, wide), BF16),
        dma((2,)), dma((2,)), dma((2, nx - 1)), dma((2, nx - 1)),
        halves, halves, dma((2 * pairs,)), dma((2 * pairs,)), vmem((rows, TILE), F32),
        halves, vmem((nx - 1, 2, xrows, wide), BF16), vmem((2, xrows, wide), F32),
        dma((2 * pairs, nx - 1)), dma((2 * pairs, nx - 1)),
        vmem((2, xrows, wide), F32), vmem((nz, tallness, LANES), BF16), vmem((nz, tallness, LANES), BF16),
        dma((nz,)), dma((nz,)), vmem((LANES, LANES), F32), vmem((2, rows, LANES), F32),
    ]
    return pl.pallas_call(
        functools.partial(kernel, dims),
        out_shape=(
            jax.ShapeDtypeStruct((rb, wide), BF16),
            jax.ShapeDtypeStruct((rows,), F32),
        ),
        in_specs=[pl.BlockSpec(memory_space=pl.ANY)] * 4,
        out_specs=(spec, spec),
        scratch_shapes=scratch,
        compiler_params=pltpu.CompilerParams(collective_id=0, has_side_effects=True),
    )(hidden, weight, targets, row_weight)


def on_mesh(split):
    dims = (split.shape["zlo"], split.shape["x"])
    tensor, pipe = ("zhi", "core"), ("zlo", "x")
    in_specs = (P(("dp", *pipe), tensor), P(None, (*pipe, *tensor)), P("dp"), P("dp"))
    out_specs = (P(("dp", *pipe), tensor), P("dp"))
    return jax.shard_map(
        functools.partial(per_device, dims), mesh=split, in_specs=in_specs, out_specs=out_specs, check_vma=False
    )


def solution(mesh):
    return on_mesh(Mesh(mesh.devices.reshape(mesh.shape["dp"], 8, 4, 2, 2), AXES))
```

```python
import functools

import jax
import jax.numpy as jnp
from jax import lax
from jax.experimental import pallas as pl
from jax.experimental.pallas import tpu as pltpu
from jax.sharding import Mesh
from jax.sharding import PartitionSpec as P

AXES = ("dp", "zlo", "x", "zhi", "core")
MESH = pl.DeviceIdType.MESH
F32 = jnp.float32
BF16 = jnp.bfloat16
LANES = 128
TILE = 256


def kernel(
    dims, h_hbm, w_hbm, t_hbm, rw_hbm, out_ref, loss_ref,
    h_ref, t_ref, rw_ref, in_sem, w_ref, w_sem, hid, pieces, tall, wide_rows, zg_s, zg_r, xg_s, xg_r, cg_s, cg_r,
    logits, soft, tcol, stat, srow, s_cx, s_z, s_loss, sc_s, sc_r, sz_s, sz_r, sl_s, sl_r,
    t_out, t_in, t_own, tx_in, tc_s, tc_r, tx_s, tx_r,
    c_out, c_in, rc_s, rc_r, whole_ref, x_out, x_in, x_own, rx_s, rx_r,
    acc, z_out, z_in, rz_s, rz_r, flat, factor,
):
    nzlo, nx = dims
    nz = 2 * nzlo
    rb, wide = h_ref.shape
    quarters = wide // LANES
    rows = nzlo * nx * rb
    xrows = nzlo * rb
    step = 48
    vocab = w_ref.shape[1]
    per_x = xrows // step
    zlo, x = lax.axis_index("zlo"), lax.axis_index("x")
    zhi, core = lax.axis_index("zhi"), lax.axis_index("core")
    z = zhi * nzlo + zlo
    other = 1 - core
    pairs = wide // TILE

    def at_z(k):
        k = lax.rem(k + nz, nz)
        return {"zhi": k // nzlo, "zlo": lax.rem(k, nzlo)}

    def at_x(k):
        return {"x": lax.rem(k, nx)}

    at_core = {"core": other}

    def remote(src, dst, send, recv, where):
        return pltpu.make_async_remote_copy(
            src_ref=src, dst_ref=dst, send_sem=send, recv_sem=recv, device_id=where, device_id_type=MESH
        )

    def rows_of(k, size):
        return pl.ds(pl.multiple_of(k * size, size), size)

    barrier = pltpu.get_barrier_semaphore()
    reach = nz // 4
    partners = [at_z(z + d) for d in range(-reach, reach + 1) if d] + [at_x(x + d) for d in range(1, nx)] + [at_core]
    for where in partners:
        pl.semaphore_signal(barrier, inc=1, device_id=where, device_id_type=MESH)
    small = [
        pltpu.make_async_copy(t_hbm, t_ref, in_sem.at[0]),
        pltpu.make_async_copy(rw_hbm, rw_ref, in_sem.at[1]),
        pltpu.make_async_copy(h_hbm, h_ref, in_sem.at[2]),
    ]
    for copy in small:
        copy.start()
    w_copy = pltpu.make_async_copy(w_hbm, w_ref, w_sem)
    w_copy.start()

    srow[...] = jnp.zeros_like(srow)
    for copy in small:
        copy.wait()
    srow[0:1, 0:rows] = t_ref[...].astype(F32).reshape(1, rows)
    srow[1:2, 0:rows] = rw_ref[...].reshape(1, rows)
    stat[...] = jnp.transpose(srow[...], (1, 0))
    for i in range(nx):
        for j in range(nzlo):
            to, of = (i * nzlo + j) * rb, (j * nx + i) * rb
            tcol[to : to + rb, :] = stat[of : of + rb, :]

    for j in range(quarters):
        tall[0, j * rb : (j + 1) * rb, :] = h_ref[:, j * LANES : (j + 1) * LANES].astype(F32)
    pieces[z] = tall[0].astype(BF16)

    offset = ((zlo * nx + x) * 4 + zhi * 2 + core) * vocab
    lane = lax.broadcasted_iota(jnp.int32, (step, LANES), 1)
    column = lax.broadcasted_iota(jnp.int32, (step, vocab), 1)

    def is_target(span):
        wanted = tcol[span, 0:1].astype(jnp.int32) - offset
        return column == wanted

    @pl.loop(0, rows // step)
    def _(r):
        span = rows_of(r, step)
        soft[span, :] = jnp.where(is_target(span), 1.0, 0.0).astype(BF16)

    def product(half, who, pair):
        first = (half * 2 + who) * wide + pair * TILE
        part = w_ref[pl.ds(pl.multiple_of(first, TILE), TILE), :]
        return lax.dot_general(soft[...], part, (((1,), (1,)), ((), ())), preferred_element_type=F32)

    def tile(pair):
        return rows_of(pair, TILE)

    def padded(r):
        first = (r // per_x) * LANES + lax.rem(r, per_x) * step
        return pl.ds(pl.multiple_of(first, 16), step)

    pl.semaphore_wait(barrier, len(partners))

    def gather_z(whose, d, n):
        k = lax.rem(whose + nz, nz)
        return remote(pieces.at[k], pieces.at[k], zg_s.at[n], zg_r.at[k], at_z(z + d))

    direct = [gather_z(z, sign * d, 2 * (reach - d) + (sign > 0)) for d in range(reach, 0, -1) for sign in (-1, 1)]
    onward = [gather_z(z - reach, d, 2 * reach + d - 1) for d in range(reach - 1, 0, -1)]
    backward = [gather_z(z + reach, -d, 3 * reach + d - 2) for d in range(reach, 0, -1)]
    for copy in direct:
        copy.start()

    w_copy.wait()

    @pl.loop(0, 2 * pairs)
    def _(n):
        half, pair = n // pairs, lax.rem(n, pairs)
        t_out[half, :, tile(pair)] = product(half, other, pair).astype(BF16)
        t_own[half, :, tile(pair)] = product(half, core, pair).astype(BF16)

    def t_core(half):
        return remote(t_out.at[half], t_in.at[half], tc_s.at[half], tc_r.at[half], at_core)

    t_core(0).start()
    t_core(1).start()

    size = min(4, nzlo)
    groups = nz // size
    grows = size * rb
    per_half = groups // 2

    def place(g, chunk_x):
        first = chunk_x * xrows + lax.rem(g, per_half) * grows
        return hid.at[(g // per_half) * 2 + core, pl.ds(pl.multiple_of(first, grows), grows), :]

    def over_x(g, d):
        return remote(place(g, x), place(g, x), xg_s.at[g, d - 1], xg_r.at[g, d - 1], at_x(x + d))

    def over_core(g, d):
        whose = lax.rem(x + d, nx)
        return remote(place(g, whose), place(g, whose), cg_s.at[g, d], cg_r.at[g, d], at_core)

    def pass_to_core(g):
        for d in range(1, nx):
            over_x(g, nx - d).wait_recv()
            over_core(g, d).start()

    def take_group(g):
        for i in range(size):
            k = g * size + i

            away = lax.rem(k - z + nz, nz)

            @pl.when((away != 0) & (away != reach) & (away != nz - reach))
            def _():
                remote(pieces.at[k], pieces.at[k], zg_s.at[0], zg_r.at[k], at_core).wait_recv()

            tall[i] = pieces[k].astype(F32)
            for j in range(quarters):
                wide_rows[i * rb : (i + 1) * rb, j * LANES : (j + 1) * LANES] = tall[i, j * rb : (j + 1) * rb, :]
        first = x * xrows + lax.rem(g, per_half) * grows
        hid[(g // per_half) * 2 + core, pl.ds(pl.multiple_of(first, grows), grows), :] = wide_rows[...].astype(BF16)
        for d in range(1, nx):
            over_x(g, d).start()
        over_core(g, 0).start()

    def in_turn(i):
        half = lax.rem(zhi + i // per_half, 2)
        return half * per_half + lax.rem(zlo // size + i, per_half)

    for source, copies in ((z - reach, onward), (z + reach, backward)):
        k = lax.rem(source + nz, nz)
        remote(pieces.at[k], pieces.at[k], zg_s.at[0], zg_r.at[k], at_core).wait_recv()
        for copy in copies:
            copy.start()

    def t_over_x(half, d):
        q = lax.rem(x + d, nx)
        return remote(
            t_own.at[half, rows_of(q, xrows), :], tx_in.at[d - 1, half], tx_s.at[half, d - 1], tx_r.at[half, d - 1], at_x(q)
        )

    for i in range(groups):
        take_group(in_turn(i))
    for half in range(2):
        t_core(half).wait_recv()

        @pl.loop(0, rows // step)
        def _(r):
            span = rows_of(r, step)
            t_own[half, span, :] = (t_own[half, span, :].astype(F32) + t_in[half, span, :].astype(F32)).astype(BF16)

    for i in range(per_half):
        pass_to_core(in_turn(i))

    def arrived(half):
        @pl.loop(0, per_half)
        def _(g):
            for d in range(nx):
                over_core(half * per_half + g, d).wait_recv()

    def half_rows(half):
        return jnp.concatenate([hid[2 * half], hid[2 * half + 1]], axis=1)

    def depth(half):
        return pl.ds(pl.multiple_of(half * 2 * wide, 2 * wide), 2 * wide)

    last = vocab // TILE * TILE
    arrived(zhi)

    @pl.loop(0, vocab // TILE)
    def _(n):
        cols = tile(n)
        logits[:, cols] = jnp.dot(half_rows(zhi), w_ref[depth(zhi), cols], preferred_element_type=F32)

    if vocab % TILE:
        logits[:, last:] = jnp.dot(half_rows(zhi), w_ref[depth(zhi), last:], preferred_element_type=F32)

    for i in range(per_half, groups):
        pass_to_core(in_turn(i))

    for half in range(2):
        for d in range(1, nx):
            t_over_x(half, d).start()

    far = 1 - zhi
    arrived(far)

    @pl.loop(0, vocab // TILE)
    def _(n):
        cols = tile(n)
        logits[:, cols] += jnp.dot(half_rows(far), w_ref[depth(far), cols], preferred_element_type=F32)

    if vocab % TILE:
        logits[:, last:] += jnp.dot(half_rows(far), w_ref[depth(far), last:], preferred_element_type=F32)

    @pl.loop(0, rows // step)
    def _(r):
        span = rows_of(r, step)
        part = logits[span, :]
        top = jnp.max(part, axis=1, keepdims=True)
        shifted = jnp.exp(part - top)
        soft[span, :] = shifted.astype(BF16)
        summed = jnp.sum(shifted, axis=1, keepdims=True)
        label = jnp.sum(jnp.where(is_target(span), part, 0.0), axis=1, keepdims=True)
        stat[padded(r), :] = jnp.where(lane == 0, top, jnp.where(lane == 1, summed, jnp.where(lane == 2, label, 0.0)))

    def joined(slots):
        tops = slots[:, 0:1, :]
        top = jnp.max(tops, axis=0)
        summed = jnp.sum(slots[:, 1:2, :] * jnp.exp(tops - top[None]), axis=0)
        return top, summed, jnp.sum(slots[:, 2:3, :], axis=0)

    flipped = jnp.transpose(stat[...], (1, 0))
    here = x * 2 + core
    s_cx[here] = flipped[0:4, :]

    def stats_cx(n):
        d, c = n // 2, n % 2
        return remote(
            s_cx.at[here], s_cx.at[here], sc_s.at[n], sc_r.at[n], {"x": lax.rem(x + d, nx), "core": lax.rem(core + c, 2)}
        )

    for n in range(1, 2 * nx):
        stats_cx(n).start()

    def to_core(half, pair):
        n = half * pairs + pair
        part = c_out.at[half, :, tile(pair)]
        return remote(part, c_in.at[half, :, tile(pair)], rc_s.at[n], rc_r.at[n], at_core)

    def for_partner(half):
        @pl.loop(0, pairs)
        def _(pair):
            c_out[half, :, tile(pair)] = product(half, other, pair).astype(BF16)
            to_core(half, pair).start()

    for_partner(0)
    stats_cx(1).wait()
    mine = s_cx[here, 0:1, :]
    theirs = s_cx[x * 2 + other, 0:1, :]
    core_top = jnp.maximum(mine, theirs)
    for k, own in enumerate((mine, theirs)):
        srow[...] = jnp.broadcast_to(jnp.exp(own - core_top), srow.shape)
        stat[...] = jnp.transpose(srow[...], (1, 0))
        for i in range(nx):
            factor[k, i * xrows : (i + 1) * xrows, :] = stat[i * LANES : i * LANES + xrows, :]

    def to_x(half, pair, d):
        q = lax.rem(x + d, nx)
        n = half * pairs + pair
        return remote(
            x_out.at[half, rows_of(q, xrows), tile(pair)], x_in.at[d - 1, half, :, tile(pair)],
            rx_s.at[n, d - 1], rx_r.at[n, d - 1], at_x(q),
        )

    def for_self(half, pair):
        whole_ref[...] = product(half, core, pair)
        to_core(half, pair).wait_recv()

        for k in range(TILE // LANES):
            lanes = pl.ds(pl.multiple_of(pair * TILE + k * LANES, LANES), LANES)
            whole = whole_ref[:, k * LANES : (k + 1) * LANES] * factor[0] + c_in[half, :, lanes].astype(F32) * factor[1]
            whole_ref[:, k * LANES : (k + 1) * LANES] = whole
            x_out[half, :, lanes] = whole.astype(BF16)

        x_own[half, :, tile(pair)] = whole_ref[rows_of(x, xrows), :]
        for d in range(1, nx):
            to_x(half, pair, d).start()

    @pl.loop(0, pairs)
    def _(pair):
        for_self(0, pair)

    for_partner(1)

    for n in range(2, 2 * nx):
        stats_cx(n).wait()
    all_top, all_sum, all_label = joined(s_cx[...])
    srow[0:1, :] = all_top
    srow[1:2, :] = all_sum
    srow[2:3, :] = all_label
    for d in range(nx):
        there = lax.rem(x + nx - d, nx) * 2
        top = jnp.maximum(s_cx[there, 0:1, :], s_cx[there + 1, 0:1, :])
        srow[4 + d : 5 + d, :] = jnp.exp(top - all_top)
    own_lanes = pl.ds(pl.multiple_of(x * LANES, LANES), LANES)
    s_z[z] = srow[0:4, own_lanes]

    def stats_z(d):
        return remote(s_z.at[z], s_z.at[z], sz_s.at[d], sz_r.at[d], at_z(z + d))

    @pl.loop(1, nz)
    def _(d):
        stats_z(d).start()

    flat[...] = jnp.transpose(srow[:, own_lanes], (1, 0))
    own_rows = rows_of(x, xrows)

    @pl.loop(0, pairs)
    def _(pair):
        for_self(1, pair)

    @pl.loop(0, 2)
    def _(half):
        for d in range(1, nx):
            for pair in range(pairs):
                to_x(half, pair, d).wait_recv()
        whole = x_own[half] * flat[0:xrows, 4:5]
        for d in range(1, nx):
            whole += x_in[d - 1, half].astype(F32) * flat[0:xrows, 4 + d : 5 + d]
        acc[half] = whole

    @pl.loop(1, nz)
    def _(d):
        stats_z(d).wait()

    top, summed, label = joined(s_z[...])
    srow[0:1, 0:LANES] = jnp.exp(s_z[z, 0:1, :] - top) / summed
    flat[...] = jnp.transpose(srow[:, 0:LANES], (1, 0))
    s_loss[x] = jnp.broadcast_to(jnp.log(summed) + top - label, (8, LANES))

    def losses(d):
        return remote(s_loss.at[x], s_loss.at[x], sl_s.at[d - 1], sl_r.at[d - 1], at_x(x + d))

    def to_z(k):
        return remote(z_out.at[k], z_in.at[z], rz_s.at[k], rz_r.at[z], at_z(k))

    @pl.loop(0, 2)
    def _(half):
        weight = tcol[own_rows, 1:2]
        hit = t_own[half, own_rows, :].astype(F32)
        for d in range(1, nx):
            t_over_x(half, d).wait_recv()
            hit += tx_in[d - 1, half].astype(F32)
        acc[half] = acc[half] * (weight * flat[0:xrows, 0:1]) - weight * hit
        for low in range(nzlo):
            slot = low % 4
            for j in range(quarters):
                tall[slot, j * rb : (j + 1) * rb, :] = acc[half, low * rb : (low + 1) * rb, j * LANES : (j + 1) * LANES]
            k = half * nzlo + low

            @pl.when(k == z)
            def _():
                tall[4] = tall[slot]

            z_out[k] = tall[slot].astype(BF16)

    to_z(lax.rem(z + nz // 2, nz)).start()
    for d in range(nz // 2 - 1, 0, -1):
        to_z(lax.rem(z + d, nz)).start()
        to_z(lax.rem(z + nz - d, nz)).start()

    for d in range(1, nx):
        losses(d).start()
    for d in range(1, nx):
        losses(d).wait()
    for i in range(nx):
        srow[0:1, i * LANES : (i + 1) * LANES] = s_loss[i, 0:1, :]
    stat[...] = jnp.transpose(srow[...], (1, 0))
    for i in range(nx):
        for j in range(nzlo):
            of, to = i * LANES + j * rb, (j * nx + i) * rb
            logits[to : to + rb, 0:LANES] = stat[of : of + rb, :]
    loss_ref[...] = jnp.transpose(logits[:, 0:LANES], (1, 0))[0:1, :].reshape(rows)

    @pl.loop(0, nz)
    def _(k):
        @pl.when(k != z)
        def _():
            remote(z_in.at[k], z_in.at[k], rz_s.at[k], rz_r.at[k], at_core).wait_recv()
            tall[4] += z_in[k].astype(F32)

    for j in range(quarters):
        out_ref[:, j * LANES : (j + 1) * LANES] = tall[4, j * rb : (j + 1) * rb, :].astype(BF16)

    @pl.loop(1, nz)
    def _(d):
        to_z(lax.rem(z + d, nz)).wait_send()

    for copy in direct + onward + backward:
        copy.wait_send()

    @pl.loop(0, groups)
    def _(g):
        over_core(g, 0).wait_send()
        for d in range(1, nx):
            over_core(g, d).wait_send()
            over_x(g, d).wait_send()

    @pl.loop(0, 2)
    def _(half):
        t_core(half).wait_send()
        for d in range(1, nx):
            t_over_x(half, d).wait_send()
        for pair in range(pairs):
            to_core(half, pair).wait_send()
            for d in range(1, nx):
                to_x(half, pair, d).wait_send()


def per_device(dims, hidden, weight, targets, row_weight):
    nzlo, nx = dims
    nz = 2 * nzlo
    rb, wide = hidden.shape
    depth, vocab = weight.shape
    rows = targets.shape[0]
    xrows = nzlo * rb
    size = min(4, nzlo)
    groups = nz // size
    tallness = rb * wide // LANES
    pairs = wide // TILE
    vmem, dma = pltpu.VMEM, pltpu.SemaphoreType.DMA
    spec = pl.BlockSpec(memory_space=pltpu.VMEM)
    halves = vmem((2, rows, wide), BF16)
    scratch = [
        vmem((rb, wide), BF16), vmem((rows,), jnp.int32), vmem((rows,), F32), dma((3,)),
        vmem((depth, vocab), BF16), dma(()),
        vmem((4, rows, wide), BF16), vmem((nz, tallness, LANES), BF16), vmem((5, tallness, LANES), F32),
        vmem((size * rb, wide), F32),
        dma((nz,)), dma((nz,)), dma((groups, nx - 1)), dma((groups, nx - 1)), dma((groups, nx)), dma((groups, nx)),
        vmem((rows, vocab), F32), vmem((rows, vocab), BF16), vmem((rows, LANES), F32),
        vmem((nx * LANES, LANES), F32), vmem((LANES, nx * LANES), F32),
        vmem((2 * nx, 4, nx * LANES), F32), vmem((nz, 4, LANES), F32), vmem((nx, 8, LANES), F32),
        dma((2 * nx,)), dma((2 * nx,)), dma((nz,)), dma((nz,)), dma((nx - 1,)), dma((nx - 1,)),
        halves, halves, halves, vmem((nx - 1, 2, xrows, wide), BF16),
        dma((2,)), dma((2,)), dma((2, nx - 1)), dma((2, nx - 1)),
        halves, halves, dma((2 * pairs,)), dma((2 * pairs,)), vmem((rows, TILE), F32),
        halves, vmem((nx - 1, 2, xrows, wide), BF16), vmem((2, xrows, wide), F32),
        dma((2 * pairs, nx - 1)), dma((2 * pairs, nx - 1)),
        vmem((2, xrows, wide), F32), vmem((nz, tallness, LANES), BF16), vmem((nz, tallness, LANES), BF16),
        dma((nz,)), dma((nz,)), vmem((LANES, LANES), F32), vmem((2, rows, LANES), F32),
    ]
    return pl.pallas_call(
        functools.partial(kernel, dims),
        out_shape=(
            pltpu.VMEM((rb, wide), BF16),
            pltpu.VMEM((rows,), F32),
        ),
        in_specs=[pl.BlockSpec(memory_space=pl.ANY)] * 4,
        out_specs=(spec, spec),
        scratch_shapes=scratch,
        compiler_params=pltpu.CompilerParams(collective_id=0, has_side_effects=True),
    )(hidden, weight, targets, row_weight)


def on_mesh(split):
    dims = (split.shape["zlo"], split.shape["x"])
    tensor, pipe = ("zhi", "core"), ("zlo", "x")
    in_specs = (P(("dp", *pipe), tensor), P(None, (*pipe, *tensor)), P("dp"), P("dp"))
    out_specs = (P(("dp", *pipe), tensor), P("dp"))
    return jax.shard_map(
        functools.partial(per_device, dims), mesh=split, in_specs=in_specs, out_specs=out_specs, check_vma=False
    )


def solution(mesh):
    return on_mesh(Mesh(mesh.devices.reshape(mesh.shape["dp"], 8, 4, 2, 2), AXES))
```

```python
import functools

import jax
import jax.numpy as jnp
from jax import lax
from jax.experimental import pallas as pl
from jax.experimental.pallas import tpu as pltpu
from jax.sharding import Mesh
from jax.sharding import PartitionSpec as P

AXES = ("dp", "zlo", "x", "zhi", "core")
MESH = pl.DeviceIdType.MESH
F32 = jnp.float32
BF16 = jnp.bfloat16
LANES = 128
TILE = 256


def kernel(
    dims, h_hbm, w_hbm, t_hbm, rw_hbm, out_ref, loss_ref,
    h_ref, t_ref, rw_ref, in_sem, w_ref, w_sem, hid, pieces, tall, wide_rows, zg_s, zg_r, xg_s, xg_r, cg_s, cg_r,
    logits, soft, tcol, stat, srow, s_cx, s_z, s_loss, sc_s, sc_r, sz_s, sz_r, sl_s, sl_r,
    t_out, t_in, t_own, tc_s, tc_r, to_in, tm_in, tm_out, to_s, to_r, tm_s, tm_r, t_rows, tx_in, tx_s, tx_r,
    c_out, c_in, rc_s, rc_r, whole_ref, x_out, x_in, x_own, rx_s, rx_r, t_wide,
    acc, z_out, z_in, rz_s, rz_r, flat, factor, own_col, tall_col,
):
    nzlo, nx = dims
    nz = 2 * nzlo
    rb, wide = h_ref.shape
    quarters = wide // LANES
    rows = nzlo * nx * rb
    xrows = nzlo * rb
    step = 48
    vocab = w_ref.shape[1]
    per_x = xrows // step
    zlo, x = lax.axis_index("zlo"), lax.axis_index("x")
    zhi, core = lax.axis_index("zhi"), lax.axis_index("core")
    z = zhi * nzlo + zlo
    other = 1 - core
    pairs = wide // TILE

    def at_z(k):
        k = lax.rem(k + nz, nz)
        return {"zhi": k // nzlo, "zlo": lax.rem(k, nzlo)}

    def at_x(k):
        return {"x": lax.rem(k, nx)}

    at_core = {"core": other}

    def remote(src, dst, send, recv, where):
        return pltpu.make_async_remote_copy(
            src_ref=src, dst_ref=dst, send_sem=send, recv_sem=recv, device_id=where, device_id_type=MESH
        )

    def rows_of(k, size):
        return pl.ds(pl.multiple_of(k * size, size), size)

    barrier = pltpu.get_barrier_semaphore()
    reach = nz // 4
    partners = [at_z(z + d) for d in range(-reach, reach + 1) if d] + [at_x(x + d) for d in range(1, nx)] + [at_core]
    for where in partners:
        pl.semaphore_signal(barrier, inc=1, device_id=where, device_id_type=MESH)
    small = [
        pltpu.make_async_copy(h_hbm, h_ref, in_sem.at[2]),
        pltpu.make_async_copy(t_hbm, t_ref, in_sem.at[0]),
        pltpu.make_async_copy(rw_hbm, rw_ref, in_sem.at[1]),
    ]
    for copy in small:
        copy.start()
    w_copy = pltpu.make_async_copy(w_hbm, w_ref, w_sem)
    w_copy.start()

    small[0].wait()
    for j in range(quarters):
        tall[0, j * rb : (j + 1) * rb, :] = h_ref[:, j * LANES : (j + 1) * LANES].astype(F32)
    pieces[z] = tall[0].astype(BF16)

    pl.semaphore_wait(barrier, len(partners))

    def gather_z(whose, d, n):
        k = lax.rem(whose + nz, nz)
        return remote(pieces.at[k], pieces.at[k], zg_s.at[n], zg_r.at[k], at_z(z + d))

    direct = [gather_z(z, sign * d, 2 * (reach - d) + (sign > 0)) for d in range(reach, 0, -1) for sign in (-1, 1)]
    onward = [gather_z(z - reach, d, 2 * reach + d - 1) for d in range(reach - 1, 0, -1)]
    backward = [gather_z(z + reach, -d, 3 * reach + d - 2) for d in range(reach, 0, -1)]
    for copy in direct:
        copy.start()

    srow[...] = jnp.zeros_like(srow)
    small[1].wait()
    small[2].wait()
    srow[0:1, 0:rows] = t_ref[...].astype(F32).reshape(1, rows)
    srow[1:2, 0:rows] = rw_ref[...].reshape(1, rows)
    stat[...] = jnp.transpose(srow[...], (1, 0))
    for i in range(nx):
        for j in range(nzlo):
            to, of = (i * nzlo + j) * rb, (j * nx + i) * rb
            tcol[to : to + rb, :] = stat[of : of + rb, :]
    own_rows = rows_of(x, xrows)
    own_col[...] = tcol[own_rows, :]

    offset = ((zlo * nx + x) * 4 + zhi * 2 + core) * vocab
    lane = lax.broadcasted_iota(jnp.int32, (step, LANES), 1)
    column = lax.broadcasted_iota(jnp.int32, (step, vocab), 1)

    def is_target(span, of=tcol):
        wanted = of[span, 0:1].astype(jnp.int32) - offset
        return column == wanted

    @pl.loop(0, rows // step)
    def _(r):
        span = rows_of(r, step)
        soft[span, :] = jnp.where(is_target(span, stat), 1.0, 0.0).astype(BF16)

    def product(half, who, pair):
        first = (half * 2 + who) * wide + pair * TILE
        part = w_ref[pl.ds(pl.multiple_of(first, TILE), TILE), :]
        return lax.dot_general(soft[...], part, (((1,), (1,)), ((), ())), preferred_element_type=F32)

    def tile(pair):
        return rows_of(pair, TILE)

    def padded(r):
        first = (r // per_x) * LANES + lax.rem(r, per_x) * step
        return pl.ds(pl.multiple_of(first, 16), step)

    w_copy.wait()

    @pl.loop(0, 2 * pairs)
    def _(n):
        half, pair = n // pairs, lax.rem(n, pairs)
        t_out[half, :, tile(pair)] = product(half, other, pair).astype(BF16)
        t_own[half, :, tile(pair)] = product(half, core, pair).astype(BF16)

    def t_core(half):
        return remote(t_out.at[half], t_in.at[half], tc_s.at[half], tc_r.at[half], at_core)

    t_core(0).start()
    t_core(1).start()

    size = min(4, nzlo)
    groups = nz // size
    grows = size * rb
    per_half = groups // 2

    def place(g, chunk_x):
        first = chunk_x * xrows + lax.rem(g, per_half) * grows
        return hid.at[(g // per_half) * 2 + core, pl.ds(pl.multiple_of(first, grows), grows), :]

    def over_x(g, d):
        return remote(place(g, x), place(g, x), xg_s.at[g, d - 1], xg_r.at[g, d - 1], at_x(x + d))

    def over_core(g, d):
        whose = lax.rem(x + d, nx)
        return remote(place(g, whose), place(g, whose), cg_s.at[g, d], cg_r.at[g, d], at_core)

    def pass_to_core(g):
        for d in range(1, nx):
            over_x(g, nx - d).wait_recv()
            over_core(g, d).start()

    def take_group(g):
        for i in range(size):
            k = g * size + i

            away = lax.rem(k - z + nz, nz)

            @pl.when((away != 0) & (away != reach) & (away != nz - reach))
            def _():
                remote(pieces.at[k], pieces.at[k], zg_s.at[0], zg_r.at[k], at_core).wait_recv()

            tall[i] = pieces[k].astype(F32)
            for j in range(quarters):
                wide_rows[i * rb : (i + 1) * rb, j * LANES : (j + 1) * LANES] = tall[i, j * rb : (j + 1) * rb, :]
        first = x * xrows + lax.rem(g, per_half) * grows
        hid[(g // per_half) * 2 + core, pl.ds(pl.multiple_of(first, grows), grows), :] = wide_rows[...].astype(BF16)
        for d in range(1, nx):
            over_x(g, d).start()
        over_core(g, 0).start()

    def in_turn(i):
        half = lax.rem(zhi + i // per_half, 2)
        return half * per_half + lax.rem(zlo // size + i, per_half)

    for source, copies in ((z - reach, onward), (z + reach, backward)):
        k = lax.rem(source + nz, nz)
        remote(pieces.at[k], pieces.at[k], zg_s.at[0], zg_r.at[k], at_core).wait_recv()
        for copy in copies:
            copy.start()

    span_z = nz // 2

    def t_block(k):
        k = lax.rem(k + nz, nz)
        return t_own.at[k // nzlo, rows_of(lax.rem(k, nzlo), nx * rb), :]

    def t_odd(sign, j):
        i = (sign + 1) // 2
        return remote(t_block(z + sign * (2 * j + 1)), to_in.at[i, j], to_s.at[i, j], to_r.at[i, j], at_z(z + sign))

    def t_main(sign, s):
        i = (sign + 1) // 2
        source = tm_out.at[i, s] if s else t_block(z + span_z)
        return remote(source, tm_in.at[i, s], tm_s.at[i, s], tm_r.at[i, s], at_z(z + 2 * sign))

    def t_gather(sign, j, s):
        t_odd(sign, j).wait_recv()
        found = to_in[(sign + 1) // 2, j].astype(F32)
        if s > (sign < 0):
            t_main(sign, s - 1).wait_recv()
            found += tm_in[(sign + 1) // 2, s - 1].astype(F32)
        return found

    def t_step(s):
        if s >= span_z // 2:
            return
        for sign in (-1, 1):
            j = span_z // 2 - s
            found = t_gather(sign, j, s) + t_block(z + sign * 2 * j)[...].astype(F32)
            tm_out[(sign + 1) // 2, s] = found.astype(BF16)
            t_main(sign, s).start()

    t_sent = [t_main(1, 0)] + [t_odd(sign, j) for j in range(span_z // 2 - 1, -1, -1) for sign in (-1, 1)]

    def t_over_x(d):
        q = lax.rem(x + d, nx)
        return remote(t_rows.at[q], tx_in.at[x], tx_s.at[d - 1], tx_r.at[d - 1], at_x(q))

    for i in range(groups):
        take_group(in_turn(i))
    for half in range(2):
        t_core(half).wait_recv()

        @pl.loop(0, rows // step)
        def _(r):
            span = rows_of(r, step)
            t_own[half, span, :] = (t_own[half, span, :].astype(F32) + t_in[half, span, :].astype(F32)).astype(BF16)

    for copy in t_sent:
        copy.start()

    for i in range(per_half):
        pass_to_core(in_turn(i))

    def arrived(half):
        @pl.loop(0, per_half)
        def _(g):
            for d in range(nx):
                over_core(half * per_half + g, d).wait_recv()

    def half_rows(half):
        return jnp.concatenate([hid[2 * half], hid[2 * half + 1]], axis=1)

    def depth(half):
        return pl.ds(pl.multiple_of(half * 2 * wide, 2 * wide), 2 * wide)

    last = vocab // TILE * TILE
    arrived(zhi)

    @pl.loop(0, vocab // TILE)
    def _(n):
        cols = tile(n)
        logits[:, cols] = jnp.dot(half_rows(zhi), w_ref[depth(zhi), cols], preferred_element_type=F32)

    if vocab % TILE:
        logits[:, last:] = jnp.dot(half_rows(zhi), w_ref[depth(zhi), last:], preferred_element_type=F32)

    for i in range(per_half, groups):
        pass_to_core(in_turn(i))
    t_step(1)

    far = 1 - zhi
    arrived(far)

    @pl.loop(0, vocab // TILE)
    def _(n):
        cols = tile(n)
        logits[:, cols] += jnp.dot(half_rows(far), w_ref[depth(far), cols], preferred_element_type=F32)

    if vocab % TILE:
        logits[:, last:] += jnp.dot(half_rows(far), w_ref[depth(far), last:], preferred_element_type=F32)

    @pl.loop(0, rows // step)
    def _(r):
        span = rows_of(r, step)
        part = logits[span, :]
        top = jnp.max(part, axis=1, keepdims=True)
        shifted = jnp.exp(part - top)
        soft[span, :] = shifted.astype(BF16)
        summed = jnp.sum(shifted, axis=1, keepdims=True)
        label = jnp.sum(jnp.where(is_target(span), part, 0.0), axis=1, keepdims=True)
        stat[padded(r), :] = jnp.where(lane == 0, top, jnp.where(lane == 1, summed, jnp.where(lane == 2, label, 0.0)))

    def joined(slots):
        tops = slots[:, 0:1, :]
        top = jnp.max(tops, axis=0)
        summed = jnp.sum(slots[:, 1:2, :] * jnp.exp(tops - top[None]), axis=0)
        return top, summed, jnp.sum(slots[:, 2:3, :], axis=0)

    flipped = jnp.transpose(stat[...], (1, 0))
    here = x * 2 + core
    s_cx[here] = flipped[0:4, :]

    def stats_cx(n):
        d, c = n // 2, n % 2
        return remote(
            s_cx.at[here], s_cx.at[here], sc_s.at[n], sc_r.at[n], {"x": lax.rem(x + d, nx), "core": lax.rem(core + c, 2)}
        )

    for n in range(1, 2 * nx):
        stats_cx(n).start()

    def to_core(half, pair):
        n = half * pairs + pair
        part = c_out.at[half, :, tile(pair)]
        return remote(part, c_in.at[half, :, tile(pair)], rc_s.at[n], rc_r.at[n], at_core)

    def for_partner(half):
        @pl.loop(0, pairs)
        def _(pair):
            c_out[half, :, tile(pair)] = product(half, other, pair).astype(BF16)
            to_core(half, pair).start()

    for_partner(0)
    t_step(2)
    stats_cx(1).wait()
    mine = s_cx[here, 0:1, :]
    theirs = s_cx[x * 2 + other, 0:1, :]
    core_top = jnp.maximum(mine, theirs)
    for k, own in enumerate((mine, theirs)):
        srow[...] = jnp.broadcast_to(jnp.exp(own - core_top), srow.shape)
        stat[...] = jnp.transpose(srow[...], (1, 0))
        for i in range(nx):
            factor[k, i * xrows : (i + 1) * xrows, :] = stat[i * LANES : i * LANES + xrows, :]

    def to_x(half, pair, d):
        q = lax.rem(x + d, nx)
        n = half * pairs + pair
        return remote(
            x_out.at[half, rows_of(q, xrows), tile(pair)], x_in.at[d - 1, half, :, tile(pair)],
            rx_s.at[n, d - 1], rx_r.at[n, d - 1], at_x(q),
        )

    def for_self(half, pair):
        whole_ref[...] = product(half, core, pair)
        to_core(half, pair).wait_recv()

        for k in range(TILE // LANES):
            lanes = pl.ds(pl.multiple_of(pair * TILE + k * LANES, LANES), LANES)
            whole = whole_ref[:, k * LANES : (k + 1) * LANES] * factor[0] + c_in[half, :, lanes].astype(F32) * factor[1]
            whole_ref[:, k * LANES : (k + 1) * LANES] = whole
            x_out[half, :, lanes] = whole.astype(BF16)

        x_own[half, :, tile(pair)] = whole_ref[rows_of(x, xrows), :]
        for d in range(1, nx):
            to_x(half, pair, d).start()

    @pl.loop(0, pairs)
    def _(pair):
        for_self(0, pair)

    for_partner(1)

    @pl.loop(0, pairs)
    def _(pair):
        for_self(1, pair)

    t_step(3)

    for n in range(2, 2 * nx):
        stats_cx(n).wait()
    all_top, all_sum, all_label = joined(s_cx[...])
    srow[0:1, :] = all_top
    srow[1:2, :] = all_sum
    srow[2:3, :] = all_label
    for d in range(nx):
        there = lax.rem(x + nx - d, nx) * 2
        top = jnp.maximum(s_cx[there, 0:1, :], s_cx[there + 1, 0:1, :])
        srow[4 + d : 5 + d, :] = jnp.exp(top - all_top)
    own_lanes = pl.ds(pl.multiple_of(x * LANES, LANES), LANES)
    s_z[z] = srow[0:4, own_lanes]

    def stats_z(d):
        return remote(s_z.at[z], s_z.at[z], sz_s.at[d], sz_r.at[d], at_z(z + d))

    @pl.loop(1, nz)
    def _(d):
        stats_z(d).start()

    flat[...] = jnp.transpose(srow[:, own_lanes], (1, 0))


    def to_z(k):
        return remote(z_out.at[k], z_in.at[z], rz_s.at[k], rz_r.at[z], at_z(k))

    def z_half(half):
        for d in range(1, nx):
            for pair in range(pairs):
                to_x(half, pair, d).wait_recv()
        whole = x_own[half] * flat[0:xrows, 4:5]
        for d in range(1, nx):
            whole += x_in[d - 1, half].astype(F32) * flat[0:xrows, 4 + d : 5 + d]
        acc[half] = whole
        for low in range(nzlo):
            slot = low % 4
            for j in range(quarters):
                tall[slot, j * rb : (j + 1) * rb, :] = acc[half, low * rb : (low + 1) * rb, j * LANES : (j + 1) * LANES]
            k = half * nzlo + low

            @pl.when(k == z)
            def _():
                tall[4] = tall[slot]

            @pl.when(k != z)
            def _():
                z_out[k] = tall[slot].astype(BF16)
                to_z(k).start()

    z_half(0)
    z_half(1)
    whole = t_block(z)[...].astype(F32)
    for sign in (-1, 1):
        whole += t_gather(sign, 0, span_z // 2)
    t_wide[...] = whole
    for i in range(nx):
        t_rows[i] = t_wide[i * rb : (i + 1) * rb, :].astype(BF16)
    for d in range(1, nx):
        t_over_x(d).start()
    tx_in[x] = t_rows[x]

    @pl.loop(1, nz)
    def _(d):
        stats_z(d).wait()

    top, summed, label = joined(s_z[...])
    for d in range(nz):
        srow[d : d + 1, 0:LANES] = jnp.exp(s_z[lax.rem(z + nz - d, nz), 0:1, :] - top) / summed
    flat[...] = jnp.transpose(srow[:, 0:LANES], (1, 0))
    for low in range(nzlo):

        @pl.when(zlo == low)
        def _():
            for j in range(quarters):
                tall_col[0, j * rb : (j + 1) * rb, :] = flat[low * rb : (low + 1) * rb, :]
                tall_col[1, j * rb : (j + 1) * rb, :] = own_col[low * rb : (low + 1) * rb, :]

    s_loss[x] = jnp.broadcast_to(jnp.log(summed) + top - label, (8, LANES))

    def losses(d):
        return remote(s_loss.at[x], s_loss.at[x], sl_s.at[d - 1], sl_r.at[d - 1], at_x(x + d))

    for d in range(1, nx):
        losses(d).start()
    for d in range(1, nx):
        losses(d).wait()
    for i in range(nx):
        srow[0:1, i * LANES : (i + 1) * LANES] = s_loss[i, 0:1, :]
    stat[...] = jnp.transpose(srow[...], (1, 0))
    for i in range(nx):
        for j in range(nzlo):
            of, to = i * LANES + j * rb, (j * nx + i) * rb
            logits[to : to + rb, 0:LANES] = stat[of : of + rb, :]
    loss_ref[...] = jnp.transpose(logits[:, 0:LANES], (1, 0))[0:1, :].reshape(rows)

    for d in range(1, nx):
        t_over_x(d).wait_recv()
    hit = tx_in[0].astype(F32)
    for i in range(1, nx):
        hit += tx_in[i].astype(F32)
    total = tall[4] * tall_col[0, :, 0:1]
    for d in range(1, nz):
        k = lax.rem(z + nz - d, nz)
        remote(z_in.at[k], z_in.at[k], rz_s.at[k], rz_r.at[k], at_core).wait_recv()
        total += z_in[k].astype(F32) * tall_col[0, :, d : d + 1]
    tall[4] = total
    for j in range(quarters):
        lanes = slice(j * LANES, (j + 1) * LANES)
        soft_part = tall[4, j * rb : (j + 1) * rb, :]
        out_ref[:, lanes] = (tall_col[1, 0:rb, 1:2] * (soft_part - hit[:, lanes])).astype(BF16)

    @pl.loop(1, nz)
    def _(d):
        to_z(lax.rem(z + d, nz)).wait_send()

    for copy in direct + onward + backward:
        copy.wait_send()
    for copy in t_sent + [t_main(sign, s) for s in range(1, span_z // 2) for sign in (-1, 1)]:
        copy.wait_send()
    for d in range(1, nx):
        t_over_x(d).wait_send()

    @pl.loop(0, groups)
    def _(g):
        over_core(g, 0).wait_send()
        for d in range(1, nx):
            over_core(g, d).wait_send()
            over_x(g, d).wait_send()

    @pl.loop(0, 2)
    def _(half):
        t_core(half).wait_send()
        for pair in range(pairs):
            to_core(half, pair).wait_send()
            for d in range(1, nx):
                to_x(half, pair, d).wait_send()


def per_device(dims, hidden, weight, targets, row_weight):
    nzlo, nx = dims
    nz = 2 * nzlo
    rb, wide = hidden.shape
    depth, vocab = weight.shape
    rows = targets.shape[0]
    xrows = nzlo * rb
    size = min(4, nzlo)
    groups = nz // size
    tallness = rb * wide // LANES
    zrows, reach = nx * rb, nz // 4
    pairs = wide // TILE
    vmem, dma = pltpu.VMEM, pltpu.SemaphoreType.DMA
    spec = pl.BlockSpec(memory_space=pltpu.VMEM)
    chain = vmem((2, reach, zrows, wide), BF16)
    halves = vmem((2, rows, wide), BF16)
    scratch = [
        vmem((rb, wide), BF16), vmem((rows,), jnp.int32), vmem((rows,), F32), dma((3,)),
        vmem((depth, vocab), BF16), dma(()),
        vmem((4, rows, wide), BF16), vmem((nz, tallness, LANES), BF16), vmem((5, tallness, LANES), F32),
        vmem((size * rb, wide), F32),
        dma((nz,)), dma((nz,)), dma((groups, nx - 1)), dma((groups, nx - 1)), dma((groups, nx)), dma((groups, nx)),
        vmem((rows, vocab), F32), vmem((rows, vocab), BF16), vmem((rows, LANES), F32),
        vmem((nx * LANES, LANES), F32), vmem((LANES, nx * LANES), F32),
        vmem((2 * nx, 4, nx * LANES), F32), vmem((nz, 4, LANES), F32), vmem((nx, 8, LANES), F32),
        dma((2 * nx,)), dma((2 * nx,)), dma((nz,)), dma((nz,)), dma((nx - 1,)), dma((nx - 1,)),
        halves, halves, halves, dma((2,)), dma((2,)),
        chain, chain, chain, dma((2, reach)), dma((2, reach)), dma((2, reach)), dma((2, reach)),
        vmem((nx, rb, wide), BF16), vmem((nx, rb, wide), BF16), dma((nx - 1,)), dma((nx - 1,)),
        halves, halves, dma((2 * pairs,)), dma((2 * pairs,)), vmem((rows, TILE), F32),
        halves, vmem((nx - 1, 2, xrows, wide), BF16), vmem((2, xrows, wide), F32),
        dma((2 * pairs, nx - 1)), dma((2 * pairs, nx - 1)), vmem((zrows, wide), F32),
        vmem((2, xrows, wide), F32), vmem((nz, tallness, LANES), BF16), vmem((nz, tallness, LANES), BF16),
        dma((nz,)), dma((nz,)), vmem((LANES, LANES), F32), vmem((2, rows, LANES), F32),
        vmem((xrows, LANES), F32), vmem((2, tallness, LANES), F32),
    ]
    return pl.pallas_call(
        functools.partial(kernel, dims),
        out_shape=(
            pltpu.VMEM((rb, wide), BF16),
            pltpu.VMEM((rows,), F32),
        ),
        in_specs=[pl.BlockSpec(memory_space=pl.ANY)] * 4,
        out_specs=(spec, spec),
        scratch_shapes=scratch,
        compiler_params=pltpu.CompilerParams(collective_id=0, has_side_effects=True),
    )(hidden, weight, targets, row_weight)


def on_mesh(split):
    dims = (split.shape["zlo"], split.shape["x"])
    tensor, pipe = ("zhi", "core"), ("zlo", "x")
    in_specs = (P(("dp", *pipe), tensor), P(None, (*pipe, *tensor)), P("dp"), P("dp"))
    out_specs = (P(("dp", *pipe), tensor), P("dp"))
    return jax.shard_map(
        functools.partial(per_device, dims), mesh=split, in_specs=in_specs, out_specs=out_specs, check_vma=False
    )


def solution(mesh):
    return on_mesh(Mesh(mesh.devices.reshape(mesh.shape["dp"], 8, 4, 2, 2), AXES))
```

```python
import functools

import jax
import jax.numpy as jnp
from jax import lax
from jax.experimental import pallas as pl
from jax.experimental.pallas import tpu as pltpu
from jax.sharding import Mesh
from jax.sharding import PartitionSpec as P

AXES = ("dp", "zlo", "x", "zhi", "core")
MESH = pl.DeviceIdType.MESH
F32 = jnp.float32
BF16 = jnp.bfloat16
LANES = 128
TILE = 256


def kernel(
    dims, h_hbm, w_hbm, t_hbm, rw_hbm, out_ref, loss_ref,
    h_ref, t_ref, rw_ref, in_sem, w_ref, w_sem, hid, pieces, tall, wide_rows, zg_s, zg_r, xg_s, xg_r, cg_s, cg_r,
    logits, soft, tcol, stat, srow, s_cx, s_z, s_loss, sc_s, sc_r, sz_s, sz_r, sl_s, sl_r,
    t_out, t_in, t_own, tc_s, tc_r, to_in, tm_in, tm_out, to_s, to_r, tm_s, tm_r, t_rows, tx_in, tx_s, tx_r,
    c_out, c_in, rc_s, rc_r, whole_ref, x_out, x_in, x_own, rx_s, rx_r, t_wide,
    acc, z_out, z_in, rz_s, rz_r, flat, factor, own_col, tall_col, spread,
):
    nzlo, nx = dims
    nz = 2 * nzlo
    rb, wide = h_ref.shape
    quarters = wide // LANES
    rows = nzlo * nx * rb
    xrows = nzlo * rb
    step = 48
    vocab = w_ref.shape[1]
    per_x = xrows // step
    zlo, x = lax.axis_index("zlo"), lax.axis_index("x")
    zhi, core = lax.axis_index("zhi"), lax.axis_index("core")
    z = zhi * nzlo + zlo
    other = 1 - core
    pairs = wide // TILE

    def at_z(k):
        k = lax.rem(k + nz, nz)
        return {"zhi": k // nzlo, "zlo": lax.rem(k, nzlo)}

    def at_x(k):
        return {"x": lax.rem(k, nx)}

    at_core = {"core": other}

    def remote(src, dst, send, recv, where):
        return pltpu.make_async_remote_copy(
            src_ref=src, dst_ref=dst, send_sem=send, recv_sem=recv, device_id=where, device_id_type=MESH
        )

    def rows_of(k, size):
        return pl.ds(pl.multiple_of(k * size, size), size)

    barrier = pltpu.get_barrier_semaphore()
    reach = nz // 4
    partners = [at_z(z + d) for d in range(-reach, reach + 1) if d] + [at_x(x + d) for d in range(1, nx)] + [at_core]
    for where in partners:
        pl.semaphore_signal(barrier, inc=1, device_id=where, device_id_type=MESH)
    small = [
        pltpu.make_async_copy(h_hbm, h_ref, in_sem.at[2]),
        pltpu.make_async_copy(t_hbm, t_ref, in_sem.at[0]),
        pltpu.make_async_copy(rw_hbm, rw_ref, in_sem.at[1]),
    ]
    for copy in small:
        copy.start()
    w_copy = pltpu.make_async_copy(w_hbm, w_ref, w_sem)
    w_copy.start()

    small[0].wait()
    for j in range(quarters):
        tall[0, j * rb : (j + 1) * rb, :] = h_ref[:, j * LANES : (j + 1) * LANES].astype(F32)
    pieces[z] = tall[0].astype(BF16)

    pl.semaphore_wait(barrier, len(partners))

    def gather_z(whose, d, n):
        k = lax.rem(whose + nz, nz)
        return remote(pieces.at[k], pieces.at[k], zg_s.at[n], zg_r.at[k], at_z(z + d))

    direct = [gather_z(z, sign * d, 2 * (reach - d) + (sign > 0)) for d in range(reach, 0, -1) for sign in (-1, 1)]
    onward = [gather_z(z - reach, d, 2 * reach + d - 1) for d in range(reach - 1, 0, -1)]
    backward = [gather_z(z + reach, -d, 3 * reach + d - 2) for d in range(reach, 0, -1)]
    for copy in direct:
        copy.start()

    srow[...] = jnp.zeros_like(srow)
    small[1].wait()
    small[2].wait()
    srow[0:1, 0:rows] = t_ref[...].astype(F32).reshape(1, rows)
    srow[1:2, 0:rows] = rw_ref[...].reshape(1, rows)
    stat[...] = jnp.transpose(srow[...], (1, 0))
    for i in range(nx):
        for j in range(nzlo):
            to, of = (i * nzlo + j) * rb, (j * nx + i) * rb
            tcol[to : to + rb, :] = stat[of : of + rb, :]
    own_rows = rows_of(x, xrows)
    own_col[...] = tcol[own_rows, :]

    offset = ((zlo * nx + x) * 4 + zhi * 2 + core) * vocab
    lane = lax.broadcasted_iota(jnp.int32, (step, LANES), 1)
    column = lax.broadcasted_iota(jnp.int32, (step, vocab), 1)

    def is_target(span, of=tcol):
        wanted = of[span, 0:1].astype(jnp.int32) - offset
        return column == wanted

    @pl.loop(0, rows // step)
    def _(r):
        span = rows_of(r, step)
        soft[span, :] = jnp.where(is_target(span, stat), 1.0, 0.0).astype(BF16)

    def product(half, who, pair):
        first = (half * 2 + who) * wide + pair * TILE
        part = w_ref[pl.ds(pl.multiple_of(first, TILE), TILE), :]
        return lax.dot_general(soft[...], part, (((1,), (1,)), ((), ())), preferred_element_type=F32)

    def tile(pair):
        return rows_of(pair, TILE)

    def padded(r):
        first = (r // per_x) * LANES + lax.rem(r, per_x) * step
        return pl.ds(pl.multiple_of(first, 16), step)

    w_copy.wait()

    @pl.loop(0, 2 * pairs)
    def _(n):
        half, pair = n // pairs, lax.rem(n, pairs)
        t_out[half, :, tile(pair)] = product(half, other, pair).astype(BF16)
        t_own[half, :, tile(pair)] = product(half, core, pair).astype(BF16)

    def t_core(half):
        return remote(t_out.at[half], t_in.at[half], tc_s.at[half], tc_r.at[half], at_core)

    t_core(0).start()
    t_core(1).start()

    size = min(4, nzlo)
    groups = nz // size
    grows = size * rb
    per_half = groups // 2

    def place(g, chunk_x):
        first = chunk_x * xrows + lax.rem(g, per_half) * grows
        return hid.at[(g // per_half) * 2 + core, pl.ds(pl.multiple_of(first, grows), grows), :]

    def over_x(g, d):
        return remote(place(g, x), place(g, x), xg_s.at[g, d - 1], xg_r.at[g, d - 1], at_x(x + d))

    def over_core(g, d):
        whose = lax.rem(x + d, nx)
        return remote(place(g, whose), place(g, whose), cg_s.at[g, d], cg_r.at[g, d], at_core)

    def pass_to_core(g):
        for d in range(1, nx):
            over_x(g, nx - d).wait_recv()
            over_core(g, d).start()

    def take_group(g):
        for i in range(size):
            k = g * size + i

            away = lax.rem(k - z + nz, nz)

            @pl.when((away != 0) & (away != reach) & (away != nz - reach))
            def _():
                remote(pieces.at[k], pieces.at[k], zg_s.at[0], zg_r.at[k], at_core).wait_recv()

            tall[i] = pieces[k].astype(F32)
            for j in range(quarters):
                wide_rows[i * rb : (i + 1) * rb, j * LANES : (j + 1) * LANES] = tall[i, j * rb : (j + 1) * rb, :]
        first = x * xrows + lax.rem(g, per_half) * grows
        hid[(g // per_half) * 2 + core, pl.ds(pl.multiple_of(first, grows), grows), :] = wide_rows[...].astype(BF16)
        for d in range(1, nx):
            over_x(g, d).start()
        over_core(g, 0).start()

    def in_turn(i):
        half = lax.rem(zhi + i // per_half, 2)
        return half * per_half + lax.rem(zlo // size + i, per_half)

    for source, copies in ((z - reach, onward), (z + reach, backward)):
        k = lax.rem(source + nz, nz)
        remote(pieces.at[k], pieces.at[k], zg_s.at[0], zg_r.at[k], at_core).wait_recv()
        for copy in copies:
            copy.start()

    span_z = nz // 2

    def t_block(k):
        k = lax.rem(k + nz, nz)
        return t_own.at[k // nzlo, rows_of(lax.rem(k, nzlo), nx * rb), :]

    def t_odd(sign, j):
        i = (sign + 1) // 2
        return remote(t_block(z + sign * (2 * j + 1)), to_in.at[i, j], to_s.at[i, j], to_r.at[i, j], at_z(z + sign))

    def t_main(sign, s):
        i = (sign + 1) // 2
        source = tm_out.at[i, s] if s else t_block(z + span_z)
        return remote(source, tm_in.at[i, s], tm_s.at[i, s], tm_r.at[i, s], at_z(z + 2 * sign))

    def t_gather(sign, j, s):
        t_odd(sign, j).wait_recv()
        found = to_in[(sign + 1) // 2, j].astype(F32)
        if s > (sign < 0):
            t_main(sign, s - 1).wait_recv()
            found += tm_in[(sign + 1) // 2, s - 1].astype(F32)
        return found

    def t_step(s):
        if s >= span_z // 2:
            return
        for sign in (-1, 1):
            j = span_z // 2 - s
            found = t_gather(sign, j, s) + t_block(z + sign * 2 * j)[...].astype(F32)
            tm_out[(sign + 1) // 2, s] = found.astype(BF16)
            t_main(sign, s).start()

    t_sent = [t_main(1, 0)] + [t_odd(sign, j) for j in range(span_z // 2 - 1, -1, -1) for sign in (-1, 1)]

    def t_over_x(d):
        q = lax.rem(x + d, nx)
        return remote(t_rows.at[q], tx_in.at[x], tx_s.at[d - 1], tx_r.at[d - 1], at_x(q))

    for i in range(groups):
        take_group(in_turn(i))
    for half in range(2):
        t_core(half).wait_recv()

        @pl.loop(0, rows // step)
        def _(r):
            span = rows_of(r, step)
            t_own[half, span, :] = (t_own[half, span, :].astype(F32) + t_in[half, span, :].astype(F32)).astype(BF16)

    for copy in t_sent:
        copy.start()

    for i in range(per_half):
        pass_to_core(in_turn(i))

    def arrived(half):
        @pl.loop(0, per_half)
        def _(g):
            for d in range(nx):
                over_core(half * per_half + g, d).wait_recv()

    def half_rows(half):
        return jnp.concatenate([hid[2 * half], hid[2 * half + 1]], axis=1)

    def depth(half):
        return pl.ds(pl.multiple_of(half * 2 * wide, 2 * wide), 2 * wide)

    last = vocab // TILE * TILE
    arrived(zhi)

    @pl.loop(0, vocab // TILE)
    def _(n):
        cols = tile(n)
        logits[:, cols] = jnp.dot(half_rows(zhi), w_ref[depth(zhi), cols], preferred_element_type=F32)

    if vocab % TILE:
        logits[:, last:] = jnp.dot(half_rows(zhi), w_ref[depth(zhi), last:], preferred_element_type=F32)

    for i in range(per_half, groups):
        pass_to_core(in_turn(i))
    t_step(1)

    far = 1 - zhi
    arrived(far)

    @pl.loop(0, vocab // TILE)
    def _(n):
        cols = tile(n)
        logits[:, cols] += jnp.dot(half_rows(far), w_ref[depth(far), cols], preferred_element_type=F32)

    if vocab % TILE:
        logits[:, last:] += jnp.dot(half_rows(far), w_ref[depth(far), last:], preferred_element_type=F32)

    @pl.loop(0, rows // step)
    def _(r):
        span = rows_of(r, step)
        part = logits[span, :]
        top = jnp.max(part, axis=1, keepdims=True)
        shifted = jnp.exp(part - top)
        soft[span, :] = shifted.astype(BF16)
        summed = jnp.sum(shifted, axis=1, keepdims=True)
        label = jnp.sum(jnp.where(is_target(span), part, 0.0), axis=1, keepdims=True)
        stat[padded(r), :] = jnp.where(lane == 0, top, jnp.where(lane == 1, summed, jnp.where(lane == 2, label, 0.0)))

    def joined(slots):
        tops = slots[:, 0:1, :]
        top = jnp.max(tops, axis=0)
        summed = jnp.sum(slots[:, 1:2, :] * jnp.exp(tops - top[None]), axis=0)
        return top, summed, jnp.sum(slots[:, 2:3, :], axis=0)

    flipped = jnp.transpose(stat[...], (1, 0))
    here = x * 2 + core
    s_cx[here] = flipped[0:4, :]

    def stats_cx(n):
        d, c = n // 2, n % 2
        return remote(
            s_cx.at[here], s_cx.at[here], sc_s.at[n], sc_r.at[n], {"x": lax.rem(x + d, nx), "core": lax.rem(core + c, 2)}
        )

    for n in range(1, 2 * nx):
        stats_cx(n).start()

    def to_core(half, pair):
        n = half * pairs + pair
        part = c_out.at[half, :, tile(pair)]
        return remote(part, c_in.at[half, :, tile(pair)], rc_s.at[n], rc_r.at[n], at_core)

    def for_partner(half):
        @pl.loop(0, pairs)
        def _(pair):
            c_out[half, :, tile(pair)] = product(half, other, pair).astype(BF16)
            to_core(half, pair).start()

    for_partner(0)
    t_step(2)
    stats_cx(1).wait()
    mine = s_cx[here, 0:1, :]
    theirs = s_cx[x * 2 + other, 0:1, :]
    core_top = jnp.maximum(mine, theirs)
    for k, own in enumerate((mine, theirs)):
        srow[...] = jnp.broadcast_to(jnp.exp(own - core_top), srow.shape)
        stat[...] = jnp.transpose(srow[...], (1, 0))
        for i in range(nx):
            factor[k, i * xrows : (i + 1) * xrows, :] = stat[i * LANES : i * LANES + xrows, :]

    def to_x(half, pair, d):
        q = lax.rem(x + d, nx)
        n = half * pairs + pair
        return remote(
            x_out.at[half, rows_of(q, xrows), tile(pair)], x_in.at[d - 1, half, :, tile(pair)],
            rx_s.at[n, d - 1], rx_r.at[n, d - 1], at_x(q),
        )

    def for_self(half, pair):
        whole_ref[...] = product(half, core, pair)
        to_core(half, pair).wait_recv()

        for k in range(TILE // LANES):
            lanes = pl.ds(pl.multiple_of(pair * TILE + k * LANES, LANES), LANES)
            whole = whole_ref[:, k * LANES : (k + 1) * LANES] * factor[0] + c_in[half, :, lanes].astype(F32) * factor[1]
            whole_ref[:, k * LANES : (k + 1) * LANES] = whole
            x_out[half, :, lanes] = whole.astype(BF16)

        x_own[half, :, tile(pair)] = whole_ref[rows_of(x, xrows), :]
        for d in range(1, nx):
            to_x(half, pair, d).start()

    @pl.loop(0, pairs)
    def _(pair):
        for_self(0, pair)

    for_partner(1)

    @pl.loop(0, pairs)
    def _(pair):
        for_self(1, pair)

    t_step(3)

    for n in range(2, 2 * nx):
        stats_cx(n).wait()
    all_top, all_sum, all_label = joined(s_cx[...])
    srow[0:1, :] = all_top
    srow[1:2, :] = all_sum
    srow[2:3, :] = all_label
    for d in range(nx):
        there = lax.rem(x + nx - d, nx) * 2
        top = jnp.maximum(s_cx[there, 0:1, :], s_cx[there + 1, 0:1, :])
        srow[4 + d : 5 + d, :] = jnp.exp(top - all_top)
    own_lanes = pl.ds(pl.multiple_of(x * LANES, LANES), LANES)
    s_z[z] = srow[0:4, own_lanes]

    def stats_z(d):
        return remote(s_z.at[z], s_z.at[z], sz_s.at[d], sz_r.at[d], at_z(z + d))

    @pl.loop(1, nz)
    def _(d):
        stats_z(d).start()

    flat[...] = jnp.transpose(srow[:, own_lanes], (1, 0))


    def to_z(k):
        return remote(z_out.at[k], z_in.at[z], rz_s.at[k], rz_r.at[z], at_z(k))

    def z_half(half):
        for d in range(1, nx):
            for pair in range(pairs):
                to_x(half, pair, d).wait_recv()
        whole = x_own[half] * flat[0:xrows, 4:5]
        for d in range(1, nx):
            whole += x_in[d - 1, half].astype(F32) * flat[0:xrows, 4 + d : 5 + d]
        acc[half] = whole
        for low in range(nzlo):
            slot = low % 4
            for j in range(quarters):
                tall[slot, j * rb : (j + 1) * rb, :] = acc[half, low * rb : (low + 1) * rb, j * LANES : (j + 1) * LANES]
            k = half * nzlo + low

            z_out[k] = tall[slot].astype(BF16)

            @pl.when(k == z)
            def _():
                tall[4] = tall[slot]

        for d in range(nz // 2, 0, -1):
            for sign in (1, -1)[: 1 + (d < nz // 2)]:
                to = lax.rem(z + sign * d + nz, nz)

                @pl.when(to // nzlo == half)
                def _():
                    to_z(to).start()

    z_half(0)
    z_half(1)
    whole = t_block(z)[...].astype(F32)
    for sign in (-1, 1):
        whole += t_gather(sign, 0, span_z // 2)
    t_wide[...] = whole
    for i in range(nx):
        t_rows[i] = t_wide[i * rb : (i + 1) * rb, :].astype(BF16)
    for d in range(1, nx):
        t_over_x(d).start()
    tx_in[x] = t_rows[x]

    @pl.loop(1, nz)
    def _(d):
        stats_z(d).wait()

    top, summed, label = joined(s_z[...])
    for d in range(nz):
        srow[d : d + 1, 0:LANES] = jnp.exp(s_z[lax.rem(z + nz - d, nz), 0:1, :] - top) / summed
    flat[...] = jnp.transpose(srow[:, 0:LANES], (1, 0))
    for low in range(nzlo):

        @pl.when(zlo == low)
        def _():
            for j in range(quarters):
                tall_col[0, j * rb : (j + 1) * rb, :] = flat[low * rb : (low + 1) * rb, :]
                tall_col[1, j * rb : (j + 1) * rb, :] = own_col[low * rb : (low + 1) * rb, :]

    s_loss[x] = jnp.broadcast_to(jnp.log(summed) + top - label, (8, LANES))

    def losses(d):
        return remote(s_loss.at[x], s_loss.at[x], sl_s.at[d - 1], sl_r.at[d - 1], at_x(x + d))

    for d in range(1, nx):
        losses(d).start()
    for d in range(nz):
        spread[d] = jnp.broadcast_to(tall_col[0, :, d : d + 1], spread.shape[1:])
    for d in range(1, nx):
        losses(d).wait()
    for i in range(nx):
        srow[0:1, i * LANES : (i + 1) * LANES] = s_loss[i, 0:1, :]
    stat[...] = jnp.transpose(srow[...], (1, 0))
    for i in range(nx):
        for j in range(nzlo):
            of, to = i * LANES + j * rb, (j * nx + i) * rb
            logits[to : to + rb, 0:LANES] = stat[of : of + rb, :]
    loss_ref[...] = jnp.transpose(logits[:, 0:LANES], (1, 0))[0:1, :].reshape(rows)

    for d in range(1, nx):
        t_over_x(d).wait_recv()
    hit = tx_in[0].astype(F32)
    for i in range(1, nx):
        hit += tx_in[i].astype(F32)
    total = tall[4] * spread[0]
    for d in range(1, nz):
        k = lax.rem(z + nz - d, nz)
        remote(z_in.at[k], z_in.at[k], rz_s.at[k], rz_r.at[k], at_core).wait_recv()
        total += z_in[k].astype(F32) * spread[d]
    tall[4] = total
    for j in range(quarters):
        lanes = slice(j * LANES, (j + 1) * LANES)
        soft_part = tall[4, j * rb : (j + 1) * rb, :]
        out_ref[:, lanes] = (tall_col[1, 0:rb, 1:2] * (soft_part - hit[:, lanes])).astype(BF16)

    @pl.loop(1, nz)
    def _(d):
        to_z(lax.rem(z + d, nz)).wait_send()

    for copy in direct + onward + backward:
        copy.wait_send()
    for copy in t_sent + [t_main(sign, s) for s in range(1, span_z // 2) for sign in (-1, 1)]:
        copy.wait_send()
    for d in range(1, nx):
        t_over_x(d).wait_send()

    @pl.loop(0, groups)
    def _(g):
        over_core(g, 0).wait_send()
        for d in range(1, nx):
            over_core(g, d).wait_send()
            over_x(g, d).wait_send()

    @pl.loop(0, 2)
    def _(half):
        t_core(half).wait_send()
        for pair in range(pairs):
            to_core(half, pair).wait_send()
            for d in range(1, nx):
                to_x(half, pair, d).wait_send()


def finish(grad, loss, grad_out, loss_out, sem):
    copies = [
        pltpu.make_async_copy(grad, grad_out, sem.at[0]),
        pltpu.make_async_copy(loss, loss_out, sem.at[1]),
    ]
    for copy in copies:
        copy.start()
    for copy in copies:
        copy.wait()


def per_device(dims, hidden, weight, targets, row_weight):
    nzlo, nx = dims
    nz = 2 * nzlo
    rb, wide = hidden.shape
    depth, vocab = weight.shape
    rows = targets.shape[0]
    xrows = nzlo * rb
    size = min(4, nzlo)
    groups = nz // size
    tallness = rb * wide // LANES
    zrows, reach = nx * rb, nz // 4
    pairs = wide // TILE
    vmem, dma = pltpu.VMEM, pltpu.SemaphoreType.DMA
    spec = pl.BlockSpec(memory_space=pltpu.VMEM)
    chain = vmem((2, reach, zrows, wide), BF16)
    halves = vmem((2, rows, wide), BF16)
    scratch = [
        vmem((rb, wide), BF16), vmem((rows,), jnp.int32), vmem((rows,), F32), dma((3,)),
        vmem((depth, vocab), BF16), dma(()),
        vmem((4, rows, wide), BF16), vmem((nz, tallness, LANES), BF16), vmem((5, tallness, LANES), F32),
        vmem((size * rb, wide), F32),
        dma((nz,)), dma((nz,)), dma((groups, nx - 1)), dma((groups, nx - 1)), dma((groups, nx)), dma((groups, nx)),
        vmem((rows, vocab), F32), vmem((rows, vocab), BF16), vmem((rows, LANES), F32),
        vmem((nx * LANES, LANES), F32), vmem((LANES, nx * LANES), F32),
        vmem((2 * nx, 4, nx * LANES), F32), vmem((nz, 4, LANES), F32), vmem((nx, 8, LANES), F32),
        dma((2 * nx,)), dma((2 * nx,)), dma((nz,)), dma((nz,)), dma((nx - 1,)), dma((nx - 1,)),
        halves, halves, halves, dma((2,)), dma((2,)),
        chain, chain, chain, dma((2, reach)), dma((2, reach)), dma((2, reach)), dma((2, reach)),
        vmem((nx, rb, wide), BF16), vmem((nx, rb, wide), BF16), dma((nx - 1,)), dma((nx - 1,)),
        halves, halves, dma((2 * pairs,)), dma((2 * pairs,)), vmem((rows, TILE), F32),
        halves, vmem((nx - 1, 2, xrows, wide), BF16), vmem((2, xrows, wide), F32),
        dma((2 * pairs, nx - 1)), dma((2 * pairs, nx - 1)), vmem((zrows, wide), F32),
        vmem((2, xrows, wide), F32), vmem((nz, tallness, LANES), BF16), vmem((nz, tallness, LANES), BF16),
        dma((nz,)), dma((nz,)), vmem((LANES, LANES), F32), vmem((2, rows, LANES), F32),
        vmem((xrows, LANES), F32), vmem((2, tallness, LANES), F32), vmem((nz, tallness, LANES), F32),
    ]
    results = pl.pallas_call(
        functools.partial(kernel, dims),
        out_shape=(
            pltpu.VMEM((rb, wide), BF16),
            pltpu.VMEM((rows,), F32),
        ),
        in_specs=[pl.BlockSpec(memory_space=pl.ANY)] * 4,
        out_specs=(spec, spec),
        scratch_shapes=scratch,
        compiler_params=pltpu.CompilerParams(collective_id=0, has_side_effects=True),
    )(hidden, weight, targets, row_weight)
    anywhere = pl.BlockSpec(memory_space=pl.ANY)
    return pl.pallas_call(
        finish,
        out_shape=(
            jax.ShapeDtypeStruct((rb, wide), BF16),
            jax.ShapeDtypeStruct((rows,), F32),
        ),
        in_specs=[anywhere, anywhere],
        out_specs=(anywhere, anywhere),
        scratch_shapes=[dma((2,))],
    )(*(pltpu.with_memory_space_constraint(result, pltpu.VMEM) for result in results))


def on_mesh(split):
    dims = (split.shape["zlo"], split.shape["x"])
    tensor, pipe = ("zhi", "core"), ("zlo", "x")
    in_specs = (P(("dp", *pipe), tensor), P(None, (*pipe, *tensor)), P("dp"), P("dp"))
    out_specs = (P(("dp", *pipe), tensor), P("dp"))
    return jax.shard_map(
        functools.partial(per_device, dims), mesh=split, in_specs=in_specs, out_specs=out_specs, check_vma=False
    )


def solution(mesh):
    return on_mesh(Mesh(mesh.devices.reshape(mesh.shape["dp"], 8, 4, 2, 2), AXES))
```

```python
import functools

import jax
import jax.numpy as jnp
from jax import lax
from jax.experimental import pallas as pl
from jax.experimental.pallas import tpu as pltpu
from jax.sharding import Mesh
from jax.sharding import PartitionSpec as P

AXES = ("dp", "zlo", "x", "zhi", "core")
MESH = pl.DeviceIdType.MESH
F32 = jnp.float32
BF16 = jnp.bfloat16
LANES = 128
TILE = 256


def kernel(
    dims, h_hbm, w_hbm, t_hbm, rw_hbm, out_ref, loss_ref,
    h_ref, t_ref, rw_ref, in_sem, w_ref, w_sem, hid, pieces, tall, wide_rows, zg_s, zg_r, xg_s, xg_r, cg_s, cg_r,
    logits, soft, tcol, stat, srow, s_cx, s_z, s_loss, sc_s, sc_r, sz_s, sz_r, sl_s, sl_r,
    t_out, t_in, t_own, tc_s, tc_r, to_in, tm_in, tm_out, to_s, to_r, tm_s, tm_r, t_rows, tx_in, tx_s, tx_r,
    c_out, c_in, rc_s, rc_r, whole_ref, x_out, x_in, x_own, rx_s, rx_r, t_wide,
    acc, z_out, z_in, rz_s, rz_r, flat, factor, own_col, tall_col, spread,
):
    nzlo, nx = dims
    nz = 2 * nzlo
    rb, wide = h_ref.shape
    quarters = wide // LANES
    rows = nzlo * nx * rb
    xrows = nzlo * rb
    step, few = 48, 16
    vocab = w_ref.shape[1]
    per_x = xrows // step
    zlo, x = lax.axis_index("zlo"), lax.axis_index("x")
    zhi, core = lax.axis_index("zhi"), lax.axis_index("core")
    z = zhi * nzlo + zlo
    other = 1 - core
    pairs = wide // TILE

    def at_z(k):
        k = lax.rem(k + nz, nz)
        return {"zhi": k // nzlo, "zlo": lax.rem(k, nzlo)}

    def at_x(k):
        return {"x": lax.rem(k, nx)}

    at_core = {"core": other}

    def remote(src, dst, send, recv, where):
        return pltpu.make_async_remote_copy(
            src_ref=src, dst_ref=dst, send_sem=send, recv_sem=recv, device_id=where, device_id_type=MESH
        )

    def rows_of(k, size):
        return pl.ds(pl.multiple_of(k * size, size), size)

    barrier = pltpu.get_barrier_semaphore()
    reach = nz // 4
    partners = [at_z(z + d) for d in range(-reach, reach + 1) if d] + [at_x(x + d) for d in range(1, nx)] + [at_core]
    for where in partners:
        pl.semaphore_signal(barrier, inc=1, device_id=where, device_id_type=MESH)
    small = [
        pltpu.make_async_copy(h_hbm, h_ref, in_sem.at[2]),
        pltpu.make_async_copy(t_hbm, t_ref, in_sem.at[0]),
        pltpu.make_async_copy(rw_hbm, rw_ref, in_sem.at[1]),
    ]
    for copy in small:
        copy.start()
    w_copy = pltpu.make_async_copy(w_hbm, w_ref, w_sem)
    w_copy.start()

    small[0].wait()
    for j in range(quarters):
        tall[0, j * rb : (j + 1) * rb, :] = h_ref[:, j * LANES : (j + 1) * LANES].astype(F32)
    pieces[z] = tall[0].astype(BF16)

    pl.semaphore_wait(barrier, len(partners))

    def gather_z(whose, d, n):
        k = lax.rem(whose + nz, nz)
        return remote(pieces.at[k], pieces.at[k], zg_s.at[n], zg_r.at[k], at_z(z + d))

    direct = [gather_z(z, sign * d, 2 * (reach - d) + (sign > 0)) for d in range(reach, 0, -1) for sign in (-1, 1)]
    onward = [gather_z(z - reach, d, 2 * reach + d - 1) for d in range(reach - 1, 0, -1)]
    backward = [gather_z(z + reach, -d, 3 * reach + d - 2) for d in range(reach, 0, -1)]
    for copy in direct:
        copy.start()

    srow[...] = jnp.zeros_like(srow)
    small[1].wait()
    small[2].wait()
    srow[0:1, 0:rows] = t_ref[...].astype(F32).reshape(1, rows)
    srow[1:2, 0:rows] = rw_ref[...].reshape(1, rows)
    stat[...] = jnp.transpose(srow[...], (1, 0))
    for i in range(nx):
        for j in range(nzlo):
            to, of = (i * nzlo + j) * rb, (j * nx + i) * rb
            tcol[to : to + rb, :] = stat[of : of + rb, :]
    own_rows = rows_of(x, xrows)
    own_col[...] = tcol[own_rows, :]

    offset = ((zlo * nx + x) * 4 + zhi * 2 + core) * vocab
    lane = lax.broadcasted_iota(jnp.int32, (few, LANES), 1)
    column = lax.broadcasted_iota(jnp.int32, (few, vocab), 1)

    def is_target(span, of=tcol):
        wanted = of[span, 0:1].astype(jnp.int32) - offset
        return column == wanted

    @pl.loop(0, rows // step)
    def _(r):
        for i in range(step // few):
            span = pl.ds(pl.multiple_of(r * step + i * few, few), few)
            soft[span, :] = jnp.where(is_target(span, stat), 1.0, 0.0).astype(BF16)

    def product(half, who, pair):
        first = (half * 2 + who) * wide + pair * TILE
        part = w_ref[pl.ds(pl.multiple_of(first, TILE), TILE), :]
        return lax.dot_general(soft[...], part, (((1,), (1,)), ((), ())), preferred_element_type=F32)

    def tile(pair):
        return rows_of(pair, TILE)

    def padded(r, more, size):
        first = (r // per_x) * LANES + lax.rem(r, per_x) * step + more
        return pl.ds(pl.multiple_of(first, 16), size)

    w_copy.wait()

    @pl.loop(0, 2 * pairs)
    def _(n):
        half, pair = n // pairs, lax.rem(n, pairs)
        t_out[half, :, tile(pair)] = product(half, other, pair).astype(BF16)
        t_own[half, :, tile(pair)] = product(half, core, pair).astype(BF16)

    def t_core(half):
        return remote(t_out.at[half], t_in.at[half], tc_s.at[half], tc_r.at[half], at_core)

    t_core(0).start()
    t_core(1).start()

    size = min(4, nzlo)
    groups = nz // size
    grows = size * rb
    per_half = groups // 2

    def place(g, chunk_x):
        first = chunk_x * xrows + lax.rem(g, per_half) * grows
        return hid.at[(g // per_half) * 2 + core, pl.ds(pl.multiple_of(first, grows), grows), :]

    def over_x(g, d):
        return remote(place(g, x), place(g, x), xg_s.at[g, d - 1], xg_r.at[g, d - 1], at_x(x + d))

    def over_core(g, d):
        whose = lax.rem(x + d, nx)
        return remote(place(g, whose), place(g, whose), cg_s.at[g, d], cg_r.at[g, d], at_core)

    def pass_to_core(g):
        for d in range(1, nx):
            over_x(g, nx - d).wait_recv()
            over_core(g, d).start()

    def take_group(g):
        for i in range(size):
            k = g * size + i

            away = lax.rem(k - z + nz, nz)

            @pl.when((away != 0) & (away != reach) & (away != nz - reach))
            def _():
                remote(pieces.at[k], pieces.at[k], zg_s.at[0], zg_r.at[k], at_core).wait_recv()

            tall[i] = pieces[k].astype(F32)
            for j in range(quarters):
                wide_rows[i * rb : (i + 1) * rb, j * LANES : (j + 1) * LANES] = tall[i, j * rb : (j + 1) * rb, :]
        first = x * xrows + lax.rem(g, per_half) * grows
        hid[(g // per_half) * 2 + core, pl.ds(pl.multiple_of(first, grows), grows), :] = wide_rows[...].astype(BF16)
        for d in range(1, nx):
            over_x(g, d).start()
        over_core(g, 0).start()

    def in_turn(i):
        half = lax.rem(zhi + i // per_half, 2)
        return half * per_half + lax.rem(zlo // size + i, per_half)

    for source, copies in ((z - reach, onward), (z + reach, backward)):
        k = lax.rem(source + nz, nz)
        remote(pieces.at[k], pieces.at[k], zg_s.at[0], zg_r.at[k], at_core).wait_recv()
        for copy in copies:
            copy.start()

    span_z = nz // 2

    def t_block(k):
        k = lax.rem(k + nz, nz)
        return t_own.at[k // nzlo, rows_of(lax.rem(k, nzlo), nx * rb), :]

    def t_odd(sign, j):
        i = (sign + 1) // 2
        return remote(t_block(z + sign * (2 * j + 1)), to_in.at[i, j], to_s.at[i, j], to_r.at[i, j], at_z(z + sign))

    def t_main(sign, s):
        i = (sign + 1) // 2
        source = tm_out.at[i, s] if s else t_block(z + span_z)
        return remote(source, tm_in.at[i, s], tm_s.at[i, s], tm_r.at[i, s], at_z(z + 2 * sign))

    def t_gather(sign, j, s):
        t_odd(sign, j).wait_recv()
        found = to_in[(sign + 1) // 2, j].astype(F32)
        if s > (sign < 0):
            t_main(sign, s - 1).wait_recv()
            found += tm_in[(sign + 1) // 2, s - 1].astype(F32)
        return found

    def t_step(s):
        if s >= span_z // 2:
            return
        for sign in (-1, 1):
            j = span_z // 2 - s
            found = t_gather(sign, j, s) + t_block(z + sign * 2 * j)[...].astype(F32)
            tm_out[(sign + 1) // 2, s] = found.astype(BF16)
            t_main(sign, s).start()

    t_sent = [t_main(1, 0)] + [t_odd(sign, j) for j in range(span_z // 2 - 1, -1, -1) for sign in (-1, 1)]

    def t_over_x(d):
        q = lax.rem(x + d, nx)
        return remote(t_rows.at[q], tx_in.at[x], tx_s.at[d - 1], tx_r.at[d - 1], at_x(q))

    for i in range(groups):
        take_group(in_turn(i))
    for half in range(2):
        t_core(half).wait_recv()

        @pl.loop(0, rows // step)
        def _(r):
            span = rows_of(r, step)
            t_own[half, span, :] = (t_own[half, span, :].astype(F32) + t_in[half, span, :].astype(F32)).astype(BF16)

    for copy in t_sent:
        copy.start()

    for i in range(per_half):
        pass_to_core(in_turn(i))

    def arrived(half):
        @pl.loop(0, per_half)
        def _(g):
            for d in range(nx):
                over_core(half * per_half + g, d).wait_recv()

    def half_rows(half):
        return jnp.concatenate([hid[2 * half], hid[2 * half + 1]], axis=1)

    def depth(half):
        return pl.ds(pl.multiple_of(half * 2 * wide, 2 * wide), 2 * wide)

    last = vocab // TILE * TILE
    arrived(zhi)

    @pl.loop(0, vocab // TILE)
    def _(n):
        cols = tile(n)
        logits[:, cols] = jnp.dot(half_rows(zhi), w_ref[depth(zhi), cols], preferred_element_type=F32)

    if vocab % TILE:
        logits[:, last:] = jnp.dot(half_rows(zhi), w_ref[depth(zhi), last:], preferred_element_type=F32)

    for i in range(per_half, groups):
        pass_to_core(in_turn(i))
    t_step(1)

    far = 1 - zhi
    arrived(far)

    @pl.loop(0, vocab // TILE)
    def _(n):
        cols = tile(n)
        logits[:, cols] += jnp.dot(half_rows(far), w_ref[depth(far), cols], preferred_element_type=F32)

    if vocab % TILE:
        logits[:, last:] += jnp.dot(half_rows(far), w_ref[depth(far), last:], preferred_element_type=F32)

    @pl.loop(0, rows // step)
    def _(r):
        for i in range(step // few):
            span = pl.ds(pl.multiple_of(r * step + i * few, few), few)
            part = logits[span, :]
            top = jnp.max(part, axis=1, keepdims=True)
            shifted = jnp.exp(part - top)
            soft[span, :] = shifted.astype(BF16)
            summed = jnp.sum(shifted, axis=1, keepdims=True)
            label = jnp.sum(jnp.where(is_target(span), part, 0.0), axis=1, keepdims=True)
            stat[padded(r, i * few, few), :] = jnp.where(
                lane == 0, top, jnp.where(lane == 1, summed, jnp.where(lane == 2, label, 0.0))
            )

    def joined(slots):
        tops = slots[:, 0:1, :]
        top = jnp.max(tops, axis=0)
        summed = jnp.sum(slots[:, 1:2, :] * jnp.exp(tops - top[None]), axis=0)
        return top, summed, jnp.sum(slots[:, 2:3, :], axis=0)

    flipped = jnp.transpose(stat[...], (1, 0))
    here = x * 2 + core
    s_cx[here] = flipped[0:4, :]

    def stats_cx(n):
        d, c = n // 2, n % 2
        return remote(
            s_cx.at[here], s_cx.at[here], sc_s.at[n], sc_r.at[n], {"x": lax.rem(x + d, nx), "core": lax.rem(core + c, 2)}
        )

    for n in range(1, 2 * nx):
        stats_cx(n).start()

    def to_core(half, pair):
        n = half * pairs + pair
        part = c_out.at[half, :, tile(pair)]
        return remote(part, c_in.at[half, :, tile(pair)], rc_s.at[n], rc_r.at[n], at_core)

    def for_partner(half):
        @pl.loop(0, pairs)
        def _(pair):
            c_out[half, :, tile(pair)] = product(half, other, pair).astype(BF16)
            to_core(half, pair).start()

    for_partner(0)
    t_step(2)
    stats_cx(1).wait()
    mine = s_cx[here, 0:1, :]
    theirs = s_cx[x * 2 + other, 0:1, :]
    core_top = jnp.maximum(mine, theirs)
    for k, own in enumerate((mine, theirs)):
        srow[...] = jnp.broadcast_to(jnp.exp(own - core_top), srow.shape)
        stat[...] = jnp.transpose(srow[...], (1, 0))
        for i in range(nx):
            factor[k, i * xrows : (i + 1) * xrows, :] = stat[i * LANES : i * LANES + xrows, :]

    def to_x(half, pair, d):
        q = lax.rem(x + d, nx)
        n = half * pairs + pair
        return remote(
            x_out.at[half, rows_of(q, xrows), tile(pair)], x_in.at[d - 1, half, :, tile(pair)],
            rx_s.at[n, d - 1], rx_r.at[n, d - 1], at_x(q),
        )

    def for_self(half, pair):
        whole_ref[...] = product(half, core, pair)
        to_core(half, pair).wait_recv()

        for k in range(TILE // LANES):
            lanes = pl.ds(pl.multiple_of(pair * TILE + k * LANES, LANES), LANES)
            whole = whole_ref[:, k * LANES : (k + 1) * LANES] * factor[0] + c_in[half, :, lanes].astype(F32) * factor[1]
            whole_ref[:, k * LANES : (k + 1) * LANES] = whole
            x_out[half, :, lanes] = whole.astype(BF16)

        x_own[half, :, tile(pair)] = whole_ref[rows_of(x, xrows), :]
        for d in sorted(range(1, nx), key=lambda d: -min(d, nx - d)):
            to_x(half, pair, d).start()

    @pl.loop(0, pairs)
    def _(pair):
        for_self(0, pair)

    for_partner(1)

    @pl.loop(0, pairs)
    def _(pair):
        for_self(1, pair)

    t_step(3)

    for n in range(2, 2 * nx):
        stats_cx(n).wait()
    all_top, all_sum, all_label = joined(s_cx[...])
    srow[0:1, :] = all_top
    srow[1:2, :] = all_sum
    srow[2:3, :] = all_label
    for d in range(nx):
        there = lax.rem(x + nx - d, nx) * 2
        top = jnp.maximum(s_cx[there, 0:1, :], s_cx[there + 1, 0:1, :])
        srow[4 + d : 5 + d, :] = jnp.exp(top - all_top)
    own_lanes = pl.ds(pl.multiple_of(x * LANES, LANES), LANES)
    s_z[z] = srow[0:4, own_lanes]

    def stats_z(d):
        return remote(s_z.at[z], s_z.at[z], sz_s.at[d], sz_r.at[d], at_z(z + d))

    @pl.loop(1, nz)
    def _(d):
        stats_z(d).start()

    flat[...] = jnp.transpose(srow[:, own_lanes], (1, 0))


    def to_z(k):
        return remote(z_out.at[k], z_in.at[z], rz_s.at[k], rz_r.at[z], at_z(k))

    def z_half(half):
        for d in range(1, nx):
            for pair in range(pairs):
                to_x(half, pair, d).wait_recv()
        whole = x_own[half] * flat[0:xrows, 4:5]
        for d in range(1, nx):
            whole += x_in[d - 1, half].astype(F32) * flat[0:xrows, 4 + d : 5 + d]
        acc[half] = whole
        for low in range(nzlo):
            slot = low % 4
            for j in range(quarters):
                tall[slot, j * rb : (j + 1) * rb, :] = acc[half, low * rb : (low + 1) * rb, j * LANES : (j + 1) * LANES]
            k = half * nzlo + low

            z_out[k] = tall[slot].astype(BF16)

            @pl.when(k == z)
            def _():
                tall[4] = tall[slot]

        for d in range(nz // 2, 0, -1):
            for sign in (1, -1)[: 1 + (d < nz // 2)]:
                to = lax.rem(z + sign * d + nz, nz)

                @pl.when(to // nzlo == half)
                def _():
                    to_z(to).start()

    z_half(0)
    z_half(1)
    whole = t_block(z)[...].astype(F32)
    for sign in (-1, 1):
        whole += t_gather(sign, 0, span_z // 2)
    t_wide[...] = whole
    for i in range(nx):
        t_rows[i] = t_wide[i * rb : (i + 1) * rb, :].astype(BF16)
    for d in range(1, nx):
        t_over_x(d).start()
    tx_in[x] = t_rows[x]

    @pl.loop(1, nz)
    def _(d):
        stats_z(d).wait()

    top, summed, label = joined(s_z[...])
    for d in range(nz):
        srow[d : d + 1, 0:LANES] = jnp.exp(s_z[lax.rem(z + nz - d, nz), 0:1, :] - top) / summed
    flat[...] = jnp.transpose(srow[:, 0:LANES], (1, 0))
    for low in range(nzlo):

        @pl.when(zlo == low)
        def _():
            for j in range(quarters):
                tall_col[0, j * rb : (j + 1) * rb, :] = flat[low * rb : (low + 1) * rb, :]
                tall_col[1, j * rb : (j + 1) * rb, :] = own_col[low * rb : (low + 1) * rb, :]

    s_loss[x] = jnp.broadcast_to(jnp.log(summed) + top - label, (8, LANES))

    def losses(d):
        return remote(s_loss.at[x], s_loss.at[x], sl_s.at[d - 1], sl_r.at[d - 1], at_x(x + d))

    for d in range(1, nx):
        losses(d).start()
    for d in range(nz):
        spread[d] = jnp.broadcast_to(tall_col[0, :, d : d + 1], spread.shape[1:])
    for copy in direct + onward + backward:
        copy.wait_send()
    for copy in t_sent + [t_main(sign, s) for s in range(1, span_z // 2) for sign in (-1, 1)]:
        copy.wait_send()

    @pl.loop(0, groups)
    def _(g):
        over_core(g, 0).wait_send()
        for d in range(1, nx):
            over_core(g, d).wait_send()
            over_x(g, d).wait_send()

    @pl.loop(0, 2)
    def _(half):
        t_core(half).wait_send()
        for pair in range(pairs):
            to_core(half, pair).wait_send()
            for d in range(1, nx):
                to_x(half, pair, d).wait_send()

    for d in range(1, nx):
        losses(d).wait()
    for i in range(nx):
        srow[0:1, i * LANES : (i + 1) * LANES] = s_loss[i, 0:1, :]
    stat[...] = jnp.transpose(srow[...], (1, 0))
    for i in range(nx):
        for j in range(nzlo):
            of, to = i * LANES + j * rb, (j * nx + i) * rb
            logits[to : to + rb, 0:LANES] = stat[of : of + rb, :]
    loss_ref[...] = jnp.transpose(logits[:, 0:LANES], (1, 0))[0:1, :].reshape(rows)

    for d in range(1, nx):
        t_over_x(d).wait_recv()
    hit = tx_in[0].astype(F32)
    for i in range(1, nx):
        hit += tx_in[i].astype(F32)
    total = tall[4] * spread[0]
    for d in range(1, nz):
        k = lax.rem(z + nz - d, nz)
        remote(z_in.at[k], z_in.at[k], rz_s.at[k], rz_r.at[k], at_core).wait_recv()
        total += z_in[k].astype(F32) * spread[d]
    tall[4] = total
    for j in range(quarters):
        lanes = slice(j * LANES, (j + 1) * LANES)
        soft_part = tall[4, j * rb : (j + 1) * rb, :]
        out_ref[:, lanes] = (tall_col[1, 0:rb, 1:2] * (soft_part - hit[:, lanes])).astype(BF16)

    for d in range(1, nx):
        t_over_x(d).wait_send()

    @pl.loop(1, nz)
    def _(d):
        to_z(lax.rem(z + d, nz)).wait_send()


def finish(grad, loss, grad_out, loss_out, sem):
    copies = [
        pltpu.make_async_copy(grad, grad_out, sem.at[0]),
        pltpu.make_async_copy(loss, loss_out, sem.at[1]),
    ]
    for copy in copies:
        copy.start()
    for copy in copies:
        copy.wait()


def per_device(dims, hidden, weight, targets, row_weight):
    nzlo, nx = dims
    nz = 2 * nzlo
    rb, wide = hidden.shape
    depth, vocab = weight.shape
    rows = targets.shape[0]
    xrows = nzlo * rb
    size = min(4, nzlo)
    groups = nz // size
    tallness = rb * wide // LANES
    zrows, reach = nx * rb, nz // 4
    pairs = wide // TILE
    vmem, dma = pltpu.VMEM, pltpu.SemaphoreType.DMA
    spec = pl.BlockSpec(memory_space=pltpu.VMEM)
    chain = vmem((2, reach, zrows, wide), BF16)
    halves = vmem((2, rows, wide), BF16)
    scratch = [
        vmem((rb, wide), BF16), vmem((rows,), jnp.int32), vmem((rows,), F32), dma((3,)),
        vmem((depth, vocab), BF16), dma(()),
        vmem((4, rows, wide), BF16), vmem((nz, tallness, LANES), BF16), vmem((5, tallness, LANES), F32),
        vmem((size * rb, wide), F32),
        dma((nz,)), dma((nz,)), dma((groups, nx - 1)), dma((groups, nx - 1)), dma((groups, nx)), dma((groups, nx)),
        vmem((rows, vocab), F32), vmem((rows, vocab), BF16), vmem((rows, LANES), F32),
        vmem((nx * LANES, LANES), F32), vmem((LANES, nx * LANES), F32),
        vmem((2 * nx, 4, nx * LANES), F32), vmem((nz, 4, LANES), F32), vmem((nx, 8, LANES), F32),
        dma((2 * nx,)), dma((2 * nx,)), dma((nz,)), dma((nz,)), dma((nx - 1,)), dma((nx - 1,)),
        halves, halves, halves, dma((2,)), dma((2,)),
        chain, chain, chain, dma((2, reach)), dma((2, reach)), dma((2, reach)), dma((2, reach)),
        vmem((nx, rb, wide), BF16), vmem((nx, rb, wide), BF16), dma((nx - 1,)), dma((nx - 1,)),
        halves, halves, dma((2 * pairs,)), dma((2 * pairs,)), vmem((rows, TILE), F32),
        halves, vmem((nx - 1, 2, xrows, wide), BF16), vmem((2, xrows, wide), F32),
        dma((2 * pairs, nx - 1)), dma((2 * pairs, nx - 1)), vmem((zrows, wide), F32),
        vmem((2, xrows, wide), F32), vmem((nz, tallness, LANES), BF16), vmem((nz, tallness, LANES), BF16),
        dma((nz,)), dma((nz,)), vmem((LANES, LANES), F32), vmem((2, rows, LANES), F32),
        vmem((xrows, LANES), F32), vmem((2, tallness, LANES), F32), vmem((nz, tallness, LANES), F32),
    ]
    results = pl.pallas_call(
        functools.partial(kernel, dims),
        out_shape=(
            pltpu.VMEM((rb, wide), BF16),
            pltpu.VMEM((rows,), F32),
        ),
        in_specs=[pl.BlockSpec(memory_space=pl.ANY)] * 4,
        out_specs=(spec, spec),
        scratch_shapes=scratch,
        compiler_params=pltpu.CompilerParams(collective_id=0, has_side_effects=True),
    )(hidden, weight, targets, row_weight)
    anywhere = pl.BlockSpec(memory_space=pl.ANY)
    return pl.pallas_call(
        finish,
        out_shape=(
            jax.ShapeDtypeStruct((rb, wide), BF16),
            jax.ShapeDtypeStruct((rows,), F32),
        ),
        in_specs=[anywhere, anywhere],
        out_specs=(anywhere, anywhere),
        scratch_shapes=[dma((2,))],
    )(*(pltpu.with_memory_space_constraint(result, pltpu.VMEM) for result in results))


def on_mesh(split):
    dims = (split.shape["zlo"], split.shape["x"])
    tensor, pipe = ("zhi", "core"), ("zlo", "x")
    in_specs = (P(("dp", *pipe), tensor), P(None, (*pipe, *tensor)), P("dp"), P("dp"))
    out_specs = (P(("dp", *pipe), tensor), P("dp"))
    return jax.shard_map(
        functools.partial(per_device, dims), mesh=split, in_specs=in_specs, out_specs=out_specs, check_vma=False
    )


def solution(mesh):
    return on_mesh(Mesh(mesh.devices.reshape(mesh.shape["dp"], 8, 4, 2, 2), AXES))
```

```python
import functools

import jax
import jax.numpy as jnp
from jax import lax
from jax.experimental import pallas as pl
from jax.experimental.pallas import tpu as pltpu
from jax.sharding import Mesh
from jax.sharding import PartitionSpec as P

AXES = ("dp", "zlo", "x", "zhi", "core")
MESH = pl.DeviceIdType.MESH
F32 = jnp.float32
BF16 = jnp.bfloat16
LANES = 128
TILE = 256


def kernel(
    dims, h_hbm, w_hbm, t_hbm, rw_hbm, out_ref, loss_ref,
    h_ref, t_ref, rw_ref, in_sem, w_ref, w_sem, hid, pieces, tall, wide_rows, zg_s, zg_r, xg_s, xg_r, cg_s, cg_r,
    logits, soft, tcol, stat, srow, s_cx, s_z, s_loss, sc_s, sc_r, sz_s, sz_r, sl_s, sl_r,
    t_out, t_in, t_own, tc_s, tc_r, to_in, tm_in, tm_out, to_s, to_r, tm_s, tm_r, t_rows, tx_in, tx_s, tx_r,
    c_out, c_in, rc_s, rc_r, whole_ref, x_out, x_in, x_own, rx_s, rx_r, t_wide,
    acc, z_out, z_in, rz_s, rz_r, flat, factor, own_col, tall_col, spread,
):
    nzlo, nx = dims
    nz = 2 * nzlo
    rb, wide = h_ref.shape
    quarters = wide // LANES
    rows = nzlo * nx * rb
    xrows = nzlo * rb
    step, few = 48, 16
    vocab = w_ref.shape[1]
    per_x = xrows // step
    zlo, x = lax.axis_index("zlo"), lax.axis_index("x")
    zhi, core = lax.axis_index("zhi"), lax.axis_index("core")
    z = zhi * nzlo + zlo
    other = 1 - core
    pairs = wide // TILE

    def at_z(k):
        k = lax.rem(k + nz, nz)
        return {"zhi": k // nzlo, "zlo": lax.rem(k, nzlo)}

    def at_x(k):
        return {"x": lax.rem(k, nx)}

    at_core = {"core": other}

    def remote(src, dst, send, recv, where):
        return pltpu.make_async_remote_copy(
            src_ref=src, dst_ref=dst, send_sem=send, recv_sem=recv, device_id=where, device_id_type=MESH
        )

    def rows_of(k, size):
        return pl.ds(pl.multiple_of(k * size, size), size)

    barrier = pltpu.get_barrier_semaphore()
    reach = nz // 4
    partners = [at_z(z + d) for d in range(-reach, reach + 1) if d] + [at_x(x + d) for d in range(1, nx)] + [at_core]
    for where in partners:
        pl.semaphore_signal(barrier, inc=1, device_id=where, device_id_type=MESH)
    small = [
        pltpu.make_async_copy(h_hbm, h_ref, in_sem.at[2]),
        pltpu.make_async_copy(t_hbm, t_ref, in_sem.at[0]),
        pltpu.make_async_copy(rw_hbm, rw_ref, in_sem.at[1]),
    ]
    for copy in small:
        copy.start()
    w_copy = pltpu.make_async_copy(w_hbm, w_ref, w_sem)
    w_copy.start()

    small[0].wait()
    for j in range(quarters):
        tall[0, j * rb : (j + 1) * rb, :] = h_ref[:, j * LANES : (j + 1) * LANES].astype(F32)
    pieces[z] = tall[0].astype(BF16)

    pl.semaphore_wait(barrier, len(partners))

    def gather_z(whose, d, n):
        k = lax.rem(whose + nz, nz)
        return remote(pieces.at[k], pieces.at[k], zg_s.at[n], zg_r.at[k], at_z(z + d))

    direct = [gather_z(z, sign * d, 2 * (reach - d) + (sign > 0)) for d in range(reach, 0, -1) for sign in (-1, 1)]
    onward = [gather_z(z - reach, d, 2 * reach + d - 1) for d in range(reach - 1, 0, -1)]
    backward = [gather_z(z + reach, -d, 3 * reach + d - 2) for d in range(reach, 0, -1)]
    for copy in direct:
        copy.start()

    srow[...] = jnp.zeros_like(srow)
    small[1].wait()
    small[2].wait()
    srow[0:1, 0:rows] = t_ref[...].astype(F32).reshape(1, rows)
    srow[1:2, 0:rows] = rw_ref[...].reshape(1, rows)
    stat[...] = jnp.transpose(srow[...], (1, 0))
    for i in range(nx):
        for j in range(nzlo):
            to, of = (i * nzlo + j) * rb, (j * nx + i) * rb
            tcol[to : to + rb, :] = stat[of : of + rb, :]
    own_rows = rows_of(x, xrows)
    own_col[...] = tcol[own_rows, :]

    offset = ((zlo * nx + x) * 4 + zhi * 2 + core) * vocab
    lane = lax.broadcasted_iota(jnp.int32, (few, LANES), 1)
    column = lax.broadcasted_iota(jnp.int32, (few, vocab), 1)

    def is_target(span, of=tcol):
        wanted = of[span, 0:1].astype(jnp.int32) - offset
        return column == wanted

    @pl.loop(0, rows // step)
    def _(r):
        for i in range(step // few):
            span = pl.ds(pl.multiple_of(r * step + i * few, few), few)
            soft[span, :] = jnp.where(is_target(span, stat), 1.0, 0.0).astype(BF16)

    def product(half, who, pair):
        first = (half * 2 + who) * wide + pair * TILE
        part = w_ref[pl.ds(pl.multiple_of(first, TILE), TILE), :]
        return lax.dot_general(soft[...], part, (((1,), (1,)), ((), ())), preferred_element_type=F32)

    def tile(pair):
        return rows_of(pair, TILE)

    def padded(r, more, size):
        first = (r // per_x) * LANES + lax.rem(r, per_x) * step + more
        return pl.ds(pl.multiple_of(first, 16), size)

    w_copy.wait()

    @pl.loop(0, 2 * pairs)
    def _(n):
        half, pair = n // pairs, lax.rem(n, pairs)
        t_out[half, :, tile(pair)] = product(half, other, pair).astype(BF16)
        t_own[half, :, tile(pair)] = product(half, core, pair).astype(BF16)

    def t_core(half):
        return remote(t_out.at[half], t_in.at[half], tc_s.at[half], tc_r.at[half], at_core)

    t_core(0).start()
    t_core(1).start()

    size = min(4, nzlo)
    groups = nz // size
    grows = size * rb
    per_half = groups // 2

    def place(g, chunk_x):
        first = chunk_x * xrows + lax.rem(g, per_half) * grows
        return hid.at[(g // per_half) * 2 + core, pl.ds(pl.multiple_of(first, grows), grows), :]

    def over_x(g, d):
        return remote(place(g, x), place(g, x), xg_s.at[g, d - 1], xg_r.at[g, d - 1], at_x(x + d))

    def over_core(g, d):
        whose = lax.rem(x + d, nx)
        return remote(place(g, whose), place(g, whose), cg_s.at[g, d], cg_r.at[g, d], at_core)

    def pass_to_core(g):
        for d in range(1, nx):
            over_x(g, nx - d).wait_recv()
            over_core(g, d).start()

    def take_group(g):
        for i in range(size):
            k = g * size + i

            away = lax.rem(k - z + nz, nz)

            @pl.when((away != 0) & (away != reach) & (away != nz - reach))
            def _():
                remote(pieces.at[k], pieces.at[k], zg_s.at[0], zg_r.at[k], at_core).wait_recv()

            tall[i] = pieces[k].astype(F32)
            for j in range(quarters):
                wide_rows[i * rb : (i + 1) * rb, j * LANES : (j + 1) * LANES] = tall[i, j * rb : (j + 1) * rb, :]
        first = x * xrows + lax.rem(g, per_half) * grows
        hid[(g // per_half) * 2 + core, pl.ds(pl.multiple_of(first, grows), grows), :] = wide_rows[...].astype(BF16)
        for d in range(1, nx):
            over_x(g, d).start()
        over_core(g, 0).start()

    def in_turn(i):
        half = lax.rem(zhi + i // per_half, 2)
        return half * per_half + lax.rem(zlo // size + i, per_half)

    for source, copies in ((z - reach, onward), (z + reach, backward)):
        k = lax.rem(source + nz, nz)
        remote(pieces.at[k], pieces.at[k], zg_s.at[0], zg_r.at[k], at_core).wait_recv()
        for copy in copies:
            copy.start()

    span_z = nz // 2

    def t_block(k):
        k = lax.rem(k + nz, nz)
        return t_own.at[k // nzlo, rows_of(lax.rem(k, nzlo), nx * rb), :]

    def t_odd(sign, j):
        i = (sign + 1) // 2
        return remote(t_block(z + sign * (2 * j + 1)), to_in.at[i, j], to_s.at[i, j], to_r.at[i, j], at_z(z + sign))

    def t_main(sign, s):
        i = (sign + 1) // 2
        source = tm_out.at[i, s] if s else t_block(z + span_z)
        return remote(source, tm_in.at[i, s], tm_s.at[i, s], tm_r.at[i, s], at_z(z + 2 * sign))

    def t_gather(sign, j, s):
        t_odd(sign, j).wait_recv()
        found = to_in[(sign + 1) // 2, j].astype(F32)
        if s > (sign < 0):
            t_main(sign, s - 1).wait_recv()
            found += tm_in[(sign + 1) // 2, s - 1].astype(F32)
        return found

    def t_step(s):
        if s >= span_z // 2:
            return
        for sign in (-1, 1):
            j = span_z // 2 - s
            found = t_gather(sign, j, s) + t_block(z + sign * 2 * j)[...].astype(F32)
            tm_out[(sign + 1) // 2, s] = found.astype(BF16)
            t_main(sign, s).start()

    t_sent = [t_main(1, 0)] + [t_odd(sign, j) for j in range(span_z // 2 - 1, -1, -1) for sign in (-1, 1)]

    def t_over_x(d):
        q = lax.rem(x + d, nx)
        return remote(t_rows.at[q], tx_in.at[x], tx_s.at[d - 1], tx_r.at[d - 1], at_x(q))

    for i in range(groups):
        take_group(in_turn(i))
    for half in range(2):
        t_core(half).wait_recv()

        @pl.loop(0, rows // step)
        def _(r):
            span = rows_of(r, step)
            t_own[half, span, :] = (t_own[half, span, :].astype(F32) + t_in[half, span, :].astype(F32)).astype(BF16)

    for copy in t_sent:
        copy.start()

    for i in range(per_half):
        pass_to_core(in_turn(i))

    def arrived(half):
        @pl.loop(0, per_half)
        def _(g):
            for d in range(nx):
                over_core(half * per_half + g, d).wait_recv()

    def half_rows(half):
        return jnp.concatenate([hid[2 * half], hid[2 * half + 1]], axis=1)

    def depth(half):
        return pl.ds(pl.multiple_of(half * 2 * wide, 2 * wide), 2 * wide)

    last = vocab // TILE * TILE
    arrived(zhi)

    @pl.loop(0, vocab // TILE)
    def _(n):
        cols = tile(n)
        logits[:, cols] = jnp.dot(half_rows(zhi), w_ref[depth(zhi), cols], preferred_element_type=F32)

    if vocab % TILE:
        logits[:, last:] = jnp.dot(half_rows(zhi), w_ref[depth(zhi), last:], preferred_element_type=F32)

    for i in range(per_half, groups):
        pass_to_core(in_turn(i))
    t_step(1)

    far = 1 - zhi
    arrived(far)

    @pl.loop(0, vocab // TILE)
    def _(n):
        cols = tile(n)
        logits[:, cols] += jnp.dot(half_rows(far), w_ref[depth(far), cols], preferred_element_type=F32)

    if vocab % TILE:
        logits[:, last:] += jnp.dot(half_rows(far), w_ref[depth(far), last:], preferred_element_type=F32)

    @pl.loop(0, rows // step)
    def _(r):
        for i in range(step // few):
            span = pl.ds(pl.multiple_of(r * step + i * few, few), few)
            part = logits[span, :]
            top = jnp.max(part, axis=1, keepdims=True)
            shifted = jnp.exp(part - top)
            soft[span, :] = shifted.astype(BF16)
            summed = jnp.sum(shifted, axis=1, keepdims=True)
            label = jnp.sum(jnp.where(is_target(span), part, 0.0), axis=1, keepdims=True)
            stat[padded(r, i * few, few), :] = jnp.where(
                lane == 0, top, jnp.where(lane == 1, summed, jnp.where(lane == 2, label, 0.0))
            )

    def joined(slots):
        tops = slots[:, 0:1, :]
        top = jnp.max(tops, axis=0)
        summed = jnp.sum(slots[:, 1:2, :] * jnp.exp(tops - top[None]), axis=0)
        return top, summed, jnp.sum(slots[:, 2:3, :], axis=0)

    flipped = jnp.transpose(stat[...], (1, 0))
    here = x * 2 + core
    s_cx[here] = flipped[0:4, :]

    def stats_cx(n):
        d, c = n // 2, n % 2
        return remote(
            s_cx.at[here], s_cx.at[here], sc_s.at[n], sc_r.at[n], {"x": lax.rem(x + d, nx), "core": lax.rem(core + c, 2)}
        )

    for n in range(1, 2 * nx):
        stats_cx(n).start()

    def to_core(half, pair):
        n = half * pairs + pair
        part = c_out.at[half, :, tile(pair)]
        return remote(part, c_in.at[half, :, tile(pair)], rc_s.at[n], rc_r.at[n], at_core)

    def for_partner(half):
        @pl.loop(0, pairs)
        def _(pair):
            c_out[half, :, tile(pair)] = product(half, other, pair).astype(BF16)
            to_core(half, pair).start()

    for_partner(0)
    t_step(2)
    stats_cx(1).wait()
    mine = s_cx[here, 0:1, :]
    theirs = s_cx[x * 2 + other, 0:1, :]
    core_top = jnp.maximum(mine, theirs)
    for k, own in enumerate((mine, theirs)):
        srow[...] = jnp.broadcast_to(jnp.exp(own - core_top), srow.shape)
        stat[...] = jnp.transpose(srow[...], (1, 0))
        for i in range(nx):
            factor[k, i * xrows : (i + 1) * xrows, :] = stat[i * LANES : i * LANES + xrows, :]

    def to_x(half, pair, d):
        q = lax.rem(x + d, nx)
        n = half * pairs + pair
        return remote(
            x_out.at[half, rows_of(q, xrows), tile(pair)], x_in.at[d - 1, half, :, tile(pair)],
            rx_s.at[n, d - 1], rx_r.at[n, d - 1], at_x(q),
        )

    def for_self(half, pair):
        whole_ref[...] = product(half, core, pair)
        to_core(half, pair).wait_recv()

        for k in range(TILE // LANES):
            lanes = pl.ds(pl.multiple_of(pair * TILE + k * LANES, LANES), LANES)
            whole = whole_ref[:, k * LANES : (k + 1) * LANES] * factor[0] + c_in[half, :, lanes].astype(F32) * factor[1]
            whole_ref[:, k * LANES : (k + 1) * LANES] = whole
            x_out[half, :, lanes] = whole.astype(BF16)

        x_own[half, :, tile(pair)] = whole_ref[rows_of(x, xrows), :]
        for d in sorted(range(1, nx), key=lambda d: -min(d, nx - d)):
            to_x(half, pair, d).start()

    @pl.loop(0, pairs)
    def _(pair):
        for_self(0, pair)

    for_partner(1)

    @pl.loop(0, pairs)
    def _(pair):
        for_self(1, pair)

    for n in range(2, 2 * nx):
        stats_cx(n).wait()
    all_top, all_sum, all_label = joined(s_cx[...])
    srow[0:1, :] = all_top
    srow[1:2, :] = all_sum
    srow[2:3, :] = all_label
    for d in range(nx):
        there = lax.rem(x + nx - d, nx) * 2
        top = jnp.maximum(s_cx[there, 0:1, :], s_cx[there + 1, 0:1, :])
        srow[4 + d : 5 + d, :] = jnp.exp(top - all_top)
    own_lanes = pl.ds(pl.multiple_of(x * LANES, LANES), LANES)
    s_z[z] = srow[0:4, own_lanes]

    def stats_z(d):
        return remote(s_z.at[z], s_z.at[z], sz_s.at[d], sz_r.at[d], at_z(z + d))

    @pl.loop(1, nz)
    def _(d):
        stats_z(d).start()

    t_step(3)

    flat[...] = jnp.transpose(srow[:, own_lanes], (1, 0))


    def to_z(k):
        return remote(z_out.at[k], z_in.at[z], rz_s.at[k], rz_r.at[z], at_z(k))

    def z_half(half):
        for d in range(1, nx):
            for pair in range(pairs):
                to_x(half, pair, d).wait_recv()
        whole = x_own[half] * flat[0:xrows, 4:5]
        for d in range(1, nx):
            whole += x_in[d - 1, half].astype(F32) * flat[0:xrows, 4 + d : 5 + d]
        acc[half] = whole
        for low in range(nzlo):
            slot = low % 4
            for j in range(quarters):
                tall[slot, j * rb : (j + 1) * rb, :] = acc[half, low * rb : (low + 1) * rb, j * LANES : (j + 1) * LANES]
            k = half * nzlo + low

            z_out[k] = tall[slot].astype(BF16)

            @pl.when(k == z)
            def _():
                tall[4] = tall[slot]

        for d in range(nz // 2, 0, -1):
            for sign in (1, -1)[: 1 + (d < nz // 2)]:
                to = lax.rem(z + sign * d + nz, nz)

                @pl.when(to // nzlo == half)
                def _():
                    to_z(to).start()

    z_half(0)
    z_half(1)
    whole = t_block(z)[...].astype(F32)
    for sign in (-1, 1):
        whole += t_gather(sign, 0, span_z // 2)
    t_wide[...] = whole
    for i in range(nx):
        t_rows[i] = t_wide[i * rb : (i + 1) * rb, :].astype(BF16)
    for d in range(1, nx):
        t_over_x(d).start()
    tx_in[x] = t_rows[x]

    @pl.loop(1, nz)
    def _(d):
        stats_z(d).wait()

    top, summed, label = joined(s_z[...])
    for d in range(nz):
        srow[d : d + 1, 0:LANES] = jnp.exp(s_z[lax.rem(z + nz - d, nz), 0:1, :] - top) / summed
    flat[...] = jnp.transpose(srow[:, 0:LANES], (1, 0))
    for low in range(nzlo):

        @pl.when(zlo == low)
        def _():
            for j in range(quarters):
                tall_col[0, j * rb : (j + 1) * rb, :] = flat[low * rb : (low + 1) * rb, :]
                tall_col[1, j * rb : (j + 1) * rb, :] = own_col[low * rb : (low + 1) * rb, :]

    s_loss[x] = jnp.broadcast_to(jnp.log(summed) + top - label, (8, LANES))

    def losses(d):
        return remote(s_loss.at[x], s_loss.at[x], sl_s.at[d - 1], sl_r.at[d - 1], at_x(x + d))

    for d in range(1, nx):
        losses(d).start()
    for d in range(nz):
        spread[d] = jnp.broadcast_to(tall_col[0, :, d : d + 1], spread.shape[1:])
    for copy in direct + onward + backward:
        copy.wait_send()
    for copy in t_sent + [t_main(sign, s) for s in range(1, span_z // 2) for sign in (-1, 1)]:
        copy.wait_send()

    @pl.loop(0, groups)
    def _(g):
        over_core(g, 0).wait_send()
        for d in range(1, nx):
            over_core(g, d).wait_send()
            over_x(g, d).wait_send()

    @pl.loop(0, 2)
    def _(half):
        t_core(half).wait_send()
        for pair in range(pairs):
            to_core(half, pair).wait_send()
            for d in range(1, nx):
                to_x(half, pair, d).wait_send()

    for d in range(1, nx):
        losses(d).wait()
    for i in range(nx):
        srow[0:1, i * LANES : (i + 1) * LANES] = s_loss[i, 0:1, :]
    stat[...] = jnp.transpose(srow[...], (1, 0))
    for i in range(nx):
        for j in range(nzlo):
            of, to = i * LANES + j * rb, (j * nx + i) * rb
            logits[to : to + rb, 0:LANES] = stat[of : of + rb, :]
    loss_ref[...] = jnp.transpose(logits[:, 0:LANES], (1, 0))[0:1, :].reshape(rows)

    for d in range(1, nx):
        t_over_x(d).wait_recv()
    hit = tx_in[0].astype(F32)
    for i in range(1, nx):
        hit += tx_in[i].astype(F32)
    total = tall[4] * spread[0]
    for d in range(1, nz):
        k = lax.rem(z + nz - d, nz)
        remote(z_in.at[k], z_in.at[k], rz_s.at[k], rz_r.at[k], at_core).wait_recv()
        total += z_in[k].astype(F32) * spread[d]
    tall[4] = total
    for j in range(quarters):
        lanes = slice(j * LANES, (j + 1) * LANES)
        soft_part = tall[4, j * rb : (j + 1) * rb, :]
        out_ref[:, lanes] = (tall_col[1, 0:rb, 1:2] * (soft_part - hit[:, lanes])).astype(BF16)

    for d in range(1, nx):
        t_over_x(d).wait_send()

    @pl.loop(1, nz)
    def _(d):
        to_z(lax.rem(z + d, nz)).wait_send()


def finish(grad, loss, grad_out, loss_out, sem):
    copies = [
        pltpu.make_async_copy(grad, grad_out, sem.at[0]),
        pltpu.make_async_copy(loss, loss_out, sem.at[1]),
    ]
    for copy in copies:
        copy.start()
    for copy in copies:
        copy.wait()


def per_device(dims, hidden, weight, targets, row_weight):
    nzlo, nx = dims
    nz = 2 * nzlo
    rb, wide = hidden.shape
    depth, vocab = weight.shape
    rows = targets.shape[0]
    xrows = nzlo * rb
    size = min(4, nzlo)
    groups = nz // size
    tallness = rb * wide // LANES
    zrows, reach = nx * rb, nz // 4
    pairs = wide // TILE
    vmem, dma = pltpu.VMEM, pltpu.SemaphoreType.DMA
    spec = pl.BlockSpec(memory_space=pltpu.VMEM)
    chain = vmem((2, reach, zrows, wide), BF16)
    halves = vmem((2, rows, wide), BF16)
    scratch = [
        vmem((rb, wide), BF16), vmem((rows,), jnp.int32), vmem((rows,), F32), dma((3,)),
        vmem((depth, vocab), BF16), dma(()),
        vmem((4, rows, wide), BF16), vmem((nz, tallness, LANES), BF16), vmem((5, tallness, LANES), F32),
        vmem((size * rb, wide), F32),
        dma((nz,)), dma((nz,)), dma((groups, nx - 1)), dma((groups, nx - 1)), dma((groups, nx)), dma((groups, nx)),
        vmem((rows, vocab), F32), vmem((rows, vocab), BF16), vmem((rows, LANES), F32),
        vmem((nx * LANES, LANES), F32), vmem((LANES, nx * LANES), F32),
        vmem((2 * nx, 4, nx * LANES), F32), vmem((nz, 4, LANES), F32), vmem((nx, 8, LANES), F32),
        dma((2 * nx,)), dma((2 * nx,)), dma((nz,)), dma((nz,)), dma((nx - 1,)), dma((nx - 1,)),
        halves, halves, halves, dma((2,)), dma((2,)),
        chain, chain, chain, dma((2, reach)), dma((2, reach)), dma((2, reach)), dma((2, reach)),
        vmem((nx, rb, wide), BF16), vmem((nx, rb, wide), BF16), dma((nx - 1,)), dma((nx - 1,)),
        halves, halves, dma((2 * pairs,)), dma((2 * pairs,)), vmem((rows, TILE), F32),
        halves, vmem((nx - 1, 2, xrows, wide), BF16), vmem((2, xrows, wide), F32),
        dma((2 * pairs, nx - 1)), dma((2 * pairs, nx - 1)), vmem((zrows, wide), F32),
        vmem((2, xrows, wide), F32), vmem((nz, tallness, LANES), BF16), vmem((nz, tallness, LANES), BF16),
        dma((nz,)), dma((nz,)), vmem((LANES, LANES), F32), vmem((2, rows, LANES), F32),
        vmem((xrows, LANES), F32), vmem((2, tallness, LANES), F32), vmem((nz, tallness, LANES), F32),
    ]
    results = pl.pallas_call(
        functools.partial(kernel, dims),
        out_shape=(
            pltpu.VMEM((rb, wide), BF16),
            pltpu.VMEM((rows,), F32),
        ),
        in_specs=[pl.BlockSpec(memory_space=pl.ANY)] * 4,
        out_specs=(spec, spec),
        scratch_shapes=scratch,
        compiler_params=pltpu.CompilerParams(collective_id=0, has_side_effects=True),
    )(hidden, weight, targets, row_weight)
    anywhere = pl.BlockSpec(memory_space=pl.ANY)
    return pl.pallas_call(
        finish,
        out_shape=(
            jax.ShapeDtypeStruct((rb, wide), BF16),
            jax.ShapeDtypeStruct((rows,), F32),
        ),
        in_specs=[anywhere, anywhere],
        out_specs=(anywhere, anywhere),
        scratch_shapes=[dma((2,))],
    )(*(pltpu.with_memory_space_constraint(result, pltpu.VMEM) for result in results))


def on_mesh(split):
    dims = (split.shape["zlo"], split.shape["x"])
    tensor, pipe = ("zhi", "core"), ("zlo", "x")
    in_specs = (P(("dp", *pipe), tensor), P(None, (*pipe, *tensor)), P("dp"), P("dp"))
    out_specs = (P(("dp", *pipe), tensor), P("dp"))
    return jax.shard_map(
        functools.partial(per_device, dims), mesh=split, in_specs=in_specs, out_specs=out_specs, check_vma=False
    )


def solution(mesh):
    return on_mesh(Mesh(mesh.devices.reshape(mesh.shape["dp"], 8, 4, 2, 2), AXES))
```
